32 devices in a mesh: mem: 4 (over z), space: 8 (over y, x, core).
Axes of the slice: x: 2, y: 2, z: 4, core: 2. Of those that a mesh axis runs over, the one named last changes fastest.
Arguments:
- ensemble: float32 [128, 16, 2048], P('mem', 'space'), may hold values from -6 to 6
- forcing: float32 [16, 2048], P('space'), may hold values from 2 to 8
- obs_cell: int32 [1024], P('space'), may hold values from 0 to 32767, as said below
- obs_value: float32 [1024], P('space'), may hold values from -8 to 8
- obs_var: float32 [1024], P('space'), may hold values from 0.5 to 2
- obs_noise: float32 [128, 1024], P('mem', 'space'), may hold values from -5 to 5
Outputs:
- analysis: float32 [128, 16, 2048], P('mem', 'space')
The draws below stay inside these ranges and needn't reach their ends.
Inputs may be any that keep to these rules, and one draw needn't show every extreme that they name: `obs_cell`: entries 128 * s to 128 * (s + 1) - 1 name cells of planes 2 * s to 2 * (s + 1) - 1, a cell of plane x and position p having index x * 2048 + p.
All inputs are finite; a program needn't handle non-finite values.
Results may differ from the reference program's by a relative error of at most 0.00018.
Values sent between devices are 32-bit elements; how exact they have to be, the bound alone decides.
No kernel may reach another device: no remote copies, remote signals or barrier semaphores. Data moves between devices by JAX's collectives and lax.ppermute only.
A program may use at most 64 MiB of HBM per device.

```python
import math
import jax
import jax.numpy as jnp
from jax import lax

PLANES_DEV = 2
PLANE = 2048
OBS_DEV = 128
FSTEPS = 4
ITERS = 6
MEMBERS = 128
NX = 16
NOBS = 1024
LOC = 4


def draw_obs_cell(key, part):
    blocks = NOBS // OBS_DEV
    slab_cells = PLANES_DEV * PLANE
    local_cells = jax.random.randint(key, (blocks, OBS_DEV), 0, slab_cells)
    starts = slab_cells * jnp.arange(blocks, dtype=jnp.int32)[:, None]
    return (local_cells + starts).reshape(NOBS).astype(jnp.int32)


def level_of(stream_key, dims, cuts, least, largest):
    factor_of = 1.0
    for dim, blocks in cuts:
        draws = jax.random.uniform(jax.random.fold_in(jax.random.fold_in(stream_key, 6), dim), (blocks,), jnp.float32, least / len(cuts), largest / len(cuts))
        factor_of = factor_of * jnp.repeat(jnp.exp(draws), dims[dim] // blocks).reshape((-1,) + (1,) * (len(dims) - 1 - dim))
    return factor_of


def scatter_about(key, dims, deviation, limit, cuts=(), held_as=jnp.bfloat16):
    entries = deviation * jax.random.normal(key, dims, jnp.float32)
    if cuts:
        entries = entries * level_of(key, dims, cuts, -0.22, 0.18)
    return jnp.clip(entries, -limit, limit).astype(held_as)


def setup_inputs(seed: int = 0) -> dict:
    keys = jax.random.split(jax.random.key(seed), 7)
    return {
        "ensemble": scatter_about(keys[0], (MEMBERS, NX, PLANE), 1.0, 6.0, ((0, 4), (1, 8)), jnp.float32),
        "forcing": jnp.clip(2.0 + 6.0 * jax.random.uniform(keys[1], (NX, PLANE), jnp.float32) ** level_of(keys[1], (NX, PLANE), ((0, 8),), -0.2, 0.2), 2.0, 8.0),
        "obs_cell": draw_obs_cell(jax.random.fold_in(keys[6], 71), 0),
        "obs_value": scatter_about(keys[3], (NOBS,), 2.0, 8.0, ((0, 8),), jnp.float32),
        "obs_var": jnp.clip(jnp.exp(math.log(2.0) - 1.3862944 * jax.random.uniform(keys[4], (NOBS,), jnp.float32) ** level_of(keys[4], (NOBS,), ((0, 8),), -0.2, 0.2)), 0.5, 2.0),
        "obs_noise": scatter_about(keys[5], (MEMBERS, NOBS), 1.0, 5.0, ((0, 4), (1, 8)), jnp.float32),
    }


time_step = 0.05
highest = lax.Precision.HIGHEST

def advance(states, forcing):
    forward_one = jnp.roll(states, -1, axis=1)
    back_one = jnp.roll(states, 1, axis=1)
    back_two = jnp.roll(states, 2, axis=1)
    return states + time_step * ((forward_one - back_two) * back_one - states + forcing)

def taper_of(planes_a, planes_b):
    spread = jnp.abs(planes_a[:, None] - planes_b[None, :])
    spread = jnp.minimum(spread, NX - spread)
    return jnp.maximum(0.0, 1.0 - spread.astype(jnp.float32) / LOC)

def chebyshev(covariance, rhs, lower_bound, upper_bound):
    center = (upper_bound + lower_bound) / 2.0
    radius = (upper_bound - lower_bound) / 2.0
    sigma_ratio = center / radius
    rho_now = 1.0 / sigma_ratio
    residual = rhs
    direction = rhs / center
    solution = jnp.zeros_like(rhs)
    for iteration in range(ITERS):
        solution = solution + direction
        if iteration < ITERS - 1:
            residual = residual - jnp.dot(covariance, direction, precision=highest)
            rho_next = 1.0 / (2.0 * sigma_ratio - rho_now)
            direction = rho_next * rho_now * direction + 2.0 * rho_next / radius * residual
            rho_now = rho_next
    return solution

def reference(ensemble, forcing, obs_cell, obs_value, obs_var, obs_noise):
    states = ensemble
    for counter in range(FSTEPS):
        states = advance(states, forcing)
    flattened = states.reshape(MEMBERS, NX * PLANE)
    observed = jnp.take(flattened, obs_cell, axis=1)
    obs_mean = lax.optimization_barrier(jnp.sum(observed, axis=0)) / MEMBERS
    obs_anom = observed - obs_mean
    obs_planes = (obs_cell // PLANE).astype(jnp.int32)
    taper_block = taper_of(obs_planes, obs_planes)
    gram_block = jnp.dot(obs_anom.T, obs_anom, precision=highest) / (MEMBERS - 1)
    covariance = taper_block * gram_block + jnp.diag(obs_var)
    lower_bound = jnp.min(obs_var)
    upper_bound = jnp.max(lax.optimization_barrier(jnp.sum(jnp.abs(covariance), axis=1)))
    mean_weight = chebyshev(covariance, obs_value - obs_mean, lower_bound, upper_bound)
    anom_rhs = (jnp.sqrt(obs_var)[None, :] * obs_noise - obs_anom).T
    anom_weight = chebyshev(covariance, anom_rhs, lower_bound, upper_bound)
    weight = anom_weight + mean_weight[:, None]
    state_mean = lax.optimization_barrier(jnp.sum(states, axis=0)) / MEMBERS
    state_anom = states - state_mean
    plane_taper = taper_of(jnp.arange(NX, dtype=jnp.int32), obs_planes)

    def plane_gain(taper_row):
        return jnp.dot(obs_anom * taper_row[None, :], weight, precision=highest)
    gain_blocks = lax.map(plane_gain, plane_taper)
    update = jnp.einsum('jxp,xjk->kxp', state_anom, gain_blocks, precision=highest) / (MEMBERS - 1)
    return states + update
```

```python
import functools

import jax
import jax.numpy as jnp
from jax import lax
from jax.experimental import pallas as pl
from jax.experimental.pallas import tpu as pltpu
from jax.sharding import PartitionSpec as P

FSTEPS = 4
ITERS = 6
LANES = 128
SUBLANES = 8

time_step = 0.05
highest = lax.Precision.HIGHEST


def from_behind(value, axis, steps):
    count = lax.axis_size(axis)
    pairs = [(source, (source + steps) % count) for source in range(count)]
    return lax.ppermute(value, axis, pairs)


def flipped(value, axis, mask):
    count = lax.axis_size(axis)
    return lax.ppermute(value, axis, [(i, i ^ mask) for i in range(count)])


def padded_2(x, sides, width):
    for axis, dim in sides:
        size, length = (lax.axis_size(axis), x.shape[dim])
        up = [(i, (i + 1) % size) for i in range(size)]
        down = [(j, i) for i, j in up]
        last = lax.slice_in_dim(x, length - width, length, axis=dim)
        initial = lax.slice_in_dim(x, 0, width, axis=dim)
        before = lax.ppermute(last, axis, up)
        after = lax.ppermute(initial, axis, down)
        x = jnp.concatenate([before, x, after], axis=dim)
    return x


def taper_of(planes_a, planes_b, planes_all, reach_planes):
    spread = jnp.abs(planes_a[:, None] - planes_b[None, :])
    spread = jnp.minimum(spread, planes_all - spread)
    return jnp.maximum(0.0, 1.0 - spread.astype(jnp.float32) / reach_planes)


def collect_band(values, along, reach_slabs):
    pieces = []
    for offset in range(-reach_slabs, reach_slabs + 1):
        if offset == 0:
            pieces.append(values)
        else:
            pieces.append(from_behind(values, "space", -offset))
    return jnp.concatenate(pieces, axis=along)


def banded(ensemble, forcing, obs_cell, obs_value, obs_var, obs_noise):
    members_dev, planes_dev, plane_cells = ensemble.shape
    obs_dev = obs_cell.shape[0]
    space_count = lax.axis_size("space")
    mem_count = lax.axis_size("mem")
    space_index = lax.axis_index("space")
    mem_index = lax.axis_index("mem")
    members = members_dev * mem_count
    planes_all = planes_dev * space_count
    reach_slabs = min(8, space_count // 4)
    reach_planes = planes_dev * reach_slabs
    band_width = reach_slabs * obs_dev
    states = ensemble
    for counter in range(FSTEPS):
        padded = padded_2(states, (("space", 1),), 2)
        forward_one = padded[:, 3 : 3 + planes_dev]
        back_one = padded[:, 1 : 1 + planes_dev]
        back_two = padded[:, 0:planes_dev]
        states = states + time_step * ((forward_one - back_two) * back_one - states + forcing)
    slab_cells = planes_dev * plane_cells
    local_cells = obs_cell - space_index * slab_cells
    observed = jnp.take(states.reshape(members_dev, slab_cells), local_cells, axis=1)
    own_planes = obs_cell // plane_cells
    own_rows = lax.all_gather(observed, "mem", axis=0, tiled=True)
    own_mean = jnp.sum(own_rows, axis=0) / members
    own_anom = own_rows - own_mean
    stacked = jnp.concatenate([own_anom, own_planes.astype(jnp.float32)[None, :]], axis=0)
    band = collect_band(stacked, 1, reach_slabs)
    context_anom = band[:members]
    context_planes = band[members].astype(jnp.int32)
    context_count = context_anom.shape[1]
    taper_block = taper_of(own_planes, context_planes, planes_all, reach_planes)
    gram_block = jnp.dot(own_anom.T, context_anom, precision=highest) / (members - 1)
    diagonal = jnp.arange(context_count)[None, :] == (band_width + jnp.arange(obs_dev))[:, None]
    covariance = taper_block * gram_block + jnp.where(diagonal, obs_var[:, None], 0.0)
    row_max = jnp.max(jnp.sum(jnp.abs(covariance), axis=1))
    var_min = jnp.min(obs_var)
    both = lax.pmax((row_max, -var_min), "space")
    upper_bound = both[0]
    lower_bound = -both[1]
    mean_rhs = obs_value - own_mean
    member_anom = lax.dynamic_slice_in_dim(own_anom, mem_index * members_dev, members_dev, 0)
    anom_rhs = (jnp.sqrt(obs_var)[None, :] * obs_noise - member_anom).T
    center = (upper_bound + lower_bound) / 2.0
    radius = (upper_bound - lower_bound) / 2.0
    sigma_ratio = center / radius
    rho_now = 1.0 / sigma_ratio
    resid_anom, resid_mean = (anom_rhs, mean_rhs)
    dir_anom, dir_mean = (anom_rhs / center, mean_rhs / center)
    anom_weight = jnp.zeros_like(anom_rhs)
    mean_weight = jnp.zeros_like(mean_rhs)
    for iteration in range(ITERS):
        anom_weight = anom_weight + dir_anom
        mean_weight = mean_weight + dir_mean
        if iteration < ITERS - 1:
            joined = jnp.concatenate([dir_anom, dir_mean[:, None]], axis=1)
            band_dirs = collect_band(joined, 0, reach_slabs)
            image = jnp.dot(covariance, band_dirs, precision=highest)
            image_anom = image[:, :-1]
            image_mean = image[:, -1]
            resid_anom = resid_anom - image_anom
            resid_mean = resid_mean - image_mean
            rho_next = 1.0 / (2.0 * sigma_ratio - rho_now)
            dir_anom = rho_next * rho_now * dir_anom + 2.0 * rho_next / radius * resid_anom
            dir_mean = rho_next * rho_now * dir_mean + 2.0 * rho_next / radius * resid_mean
            rho_now = rho_next
    weight = anom_weight + mean_weight[:, None]
    owned_cells = lax.all_to_all(states, "mem", split_axis=2, concat_axis=0, tiled=True)
    weight_rows = lax.all_gather(weight, "mem", axis=1, tiled=True)
    weight_context = collect_band(weight_rows, 0, reach_slabs)
    own_plane_ids = space_index * planes_dev + jnp.arange(planes_dev, dtype=jnp.int32)
    plane_taper = taper_of(own_plane_ids, context_planes, planes_all, reach_planes)

    def plane_gain(taper_row):
        return jnp.dot(context_anom * taper_row[None, :], weight_context, precision=highest)

    gain_blocks = lax.map(plane_gain, plane_taper)
    state_mean = jnp.sum(owned_cells, axis=0) / members
    state_anom = owned_cells - state_mean
    update = jnp.einsum("jxp,xjk->kxp", state_anom, gain_blocks, precision=highest) / (members - 1)
    analysis = owned_cells + update
    return lax.all_to_all(analysis, "mem", split_axis=0, concat_axis=2, tiled=True)


def halves(x):
    high = x.astype(jnp.bfloat16)
    low = (x - high.astype(jnp.float32)).astype(jnp.bfloat16)
    return high, low


def mxu(a, b):
    return jnp.dot(a, b, preferred_element_type=jnp.float32)


def round_up(value, unit):
    return -(-value // unit) * unit


def pack_kernel(ens_ref, forcing_ref, out_ref):
    members_dev, planes_dev, cells = ens_ref.shape
    blocks, rows, width = out_ref.shape
    state_rows = planes_dev * members_dev
    for block in range(blocks):
        span = slice(block * width, (block + 1) * width)
        for plane in range(planes_dev):
            top = plane * members_dev
            out_ref[block, top : top + members_dev, :] = ens_ref[:, plane, span]
        tail = jnp.zeros((rows - state_rows - planes_dev, width), jnp.float32)
        out_ref[block, state_rows:, :] = jnp.concatenate([forcing_ref[:, span], tail], axis=0)


def forecast_kernel(in_ref, out_ref, *, planes_dev, members_dev):
    blocks, rows, width = out_ref.shape
    count = blocks * planes_dev
    for lane in range(0, width, LANES):
        lanes = slice(lane, lane + LANES)
        drive = []
        for plane in range(count):
            row = rows + plane % planes_dev
            drive.append(in_ref[plane // planes_dev, row : row + 1, lanes])
        for member in range(0, members_dev, SUBLANES):
            column = []
            for plane in range(count):
                top = (plane % planes_dev) * members_dev + member
                column.append(in_ref[plane // planes_dev, top : top + SUBLANES, lanes])
            for step in range(FSTEPS):
                column = [
                    column[n]
                    + time_step
                    * (
                        (column[(n + 1) % count] - column[n - 2]) * column[n - 1]
                        - column[n]
                        + drive[n]
                    )
                    for n in range(count)
                ]
            for plane in range(count):
                top = (plane % planes_dev) * members_dev + member
                out_ref[plane // planes_dev, top : top + SUBLANES, lanes] = column[plane]


def observe_kernel(state_ref, cell_ref, out_ref, *, planes_dev, members_dev, plane_cells):
    blocks, rows, width = state_ref.shape
    obs_dev = cell_ref.shape[1]
    first = lax.axis_index("space") * (planes_dev * plane_cells)
    local = cell_ref[...] - first
    total = jnp.zeros((3 * members_dev, obs_dev), jnp.float32)
    for block in range(blocks):
        for plane in range(planes_dev):
            base = plane * plane_cells + block * width
            index = lax.broadcasted_iota(jnp.int32, (width, obs_dev), 0) + base
            pick = (index == local).astype(jnp.float32).astype(jnp.bfloat16)
            top = plane * members_dev
            values = state_ref[block, top : top + members_dev, :]
            high, rest = values.astype(jnp.bfloat16), None
            rest = values - high.astype(jnp.float32)
            middle, low = halves(rest)
            total += mxu(jnp.concatenate([high, middle, low], axis=0), pick)
    out_ref[...] = (
        total[:members_dev]
        + total[members_dev : 2 * members_dev]
        + total[2 * members_dev :]
    )


def solve_kernel(*refs, members, members_dev, planes_dev, pair, reach_slabs):
    slabs = len(refs) - 10
    ins, gain_ref = refs[:slabs], refs[slabs]
    anom_ref, flip_ref, side_ref, cov_hi, cov_lo, dir_ref, res_ref, sol_ref, split_ref = refs[
        slabs + 1 :
    ]
    obs_dev = ins[0].shape[1]
    count = slabs * obs_dev
    planes_all = planes_dev * slabs
    reach_planes = planes_dev * reach_slabs
    me = lax.axis_index("space")
    member_count = jnp.float32(members)

    for offset in range(slabs):
        slab = jnp.bitwise_xor(me, offset)
        block = ins[offset][...]
        observed = block[:members]
        mean = jnp.sum(observed, axis=0, keepdims=True) / member_count
        anom = observed - mean
        high, low = halves(anom)
        anom_ref[slab, :members] = high
        anom_ref[slab, members : 2 * members] = high
        anom_ref[slab, 2 * members :] = low
        turned = anom.T
        turned_hi, turned_lo = halves(turned)
        flip_ref[slab, :, :members] = turned_hi
        flip_ref[slab, :, members:] = turned_lo
        res_ref[slab] = block[members : members + members_dev] - observed[:members_dev]
        side_ref[slab] = block[members + members_dev : members + members_dev + SUBLANES]

    lower = None
    variances, places, columns = [], [], []
    for slab in range(slabs):
        side = side_ref[slab]
        variances.append(side[0:1])
        places.append(side[1:2])
        columns.append(side.T[:, 1:2])
    var_row = jnp.concatenate(variances, axis=1)
    place_row = jnp.concatenate(places, axis=1)
    lower = jnp.min(var_row, axis=1, keepdims=True)

    tile = pair * obs_dev
    tiles = slabs // pair
    reach_tiles = -(-reach_slabs // pair)
    near = {}
    for right in range(tiles):
        near[right] = sorted({(right + step) % tiles for step in range(-reach_tiles, reach_tiles + 1)})
    scale = jnp.float32(1.0 / (members - 1))
    upper = None
    for right in range(tiles):
        span = slice(right * tile, (right + 1) * tile)
        tops = jnp.concatenate(
            [anom_ref[right * pair + n, : 2 * members] for n in range(pair)], axis=1
        )
        lows = jnp.concatenate(
            [anom_ref[right * pair + n, 2 * members :] for n in range(pair)], axis=1
        )
        along = place_row[:, span]
        sums = None
        for order, left in enumerate(near[right]):
            for part in range(pair):
                slab = left * pair + part
                rows = flip_ref[slab]
                gram = mxu(rows, tops) + mxu(rows[:, :members], lows)
                spread = jnp.abs(columns[slab] - along)
                spread = jnp.minimum(spread, planes_all - spread)
                taper = jnp.maximum(0.0, 1.0 - spread / reach_planes)
                cov = taper * (gram * scale)
                if left == right:
                    below = lax.broadcasted_iota(jnp.int32, (obs_dev, tile), 0) + part * obs_dev
                    across = lax.broadcasted_iota(jnp.int32, (obs_dev, tile), 1)
                    cov = cov + jnp.where(below == across, var_row[:, span], 0.0)
                size = jnp.sum(jnp.abs(cov), axis=0, keepdims=True)
                sums = size if sums is None else sums + size
                high, low = halves(cov)
                top = (order * pair + part) * obs_dev
                cov_hi[right, top : top + obs_dev, :] = high
                cov_lo[right, top : top + obs_dev, :] = low
        biggest = jnp.max(sums, axis=1, keepdims=True)
        upper = biggest if upper is None else jnp.maximum(upper, biggest)

    center = (upper + lower) / 2.0
    radius = (upper - lower) / 2.0
    sigma_ratio = center / radius
    rho_now = 1.0 / sigma_ratio
    for slab in range(slabs):
        span = slice(slab * obs_dev, (slab + 1) * obs_dev)
        start = res_ref[slab] / center
        dir_ref[slab] = start
        sol_ref[slab] = start
        high, low = halves(start)
        split_ref[:members_dev, span] = high
        split_ref[members_dev:, span] = low
    for iteration in range(ITERS - 1):
        rho_next = 1.0 / (2.0 * sigma_ratio - rho_now)
        keep = rho_next * rho_now
        take = 2.0 * rho_next / radius
        images = []
        for right in range(tiles):
            lefts = jnp.concatenate(
                [split_ref[:, left * tile : (left + 1) * tile] for left in near[right]], axis=1
            )
            both = mxu(lefts, cov_hi[right])
            images.append(
                both[:members_dev]
                + both[members_dev:]
                + mxu(lefts[:members_dev], cov_lo[right])
            )
        for slab in range(slabs):
            span = slice(slab * obs_dev, (slab + 1) * obs_dev)
            part = slab % pair
            image = images[slab // pair][:, part * obs_dev : (part + 1) * obs_dev]
            residual = res_ref[slab] - image
            res_ref[slab] = residual
            ahead = keep * dir_ref[slab] + take * residual
            dir_ref[slab] = ahead
            sol_ref[slab] += ahead
            if iteration < ITERS - 2:
                high, low = halves(ahead)
                split_ref[:members_dev, span] = high
                split_ref[members_dev:, span] = low
        rho_now = rho_next

    total = jnp.zeros((2 * planes_dev * members_dev, members), jnp.float32)
    extra = jnp.zeros((planes_dev * members_dev, members), jnp.float32)
    for slab in range(slabs):
        weight = sol_ref[slab]
        tapered = []
        for plane in range(planes_dev):
            own = (me * planes_dev + plane).astype(jnp.float32)
            spread = jnp.abs(own - place_row[:, slab * obs_dev : (slab + 1) * obs_dev])
            spread = jnp.minimum(spread, planes_all - spread)
            tapered.append(weight * jnp.maximum(0.0, 1.0 - spread / reach_planes))
        high, low = halves(jnp.concatenate(tapered, axis=0))
        rows = flip_ref[slab]
        total += mxu(jnp.concatenate([high, low], axis=0), rows[:, :members])
        extra += mxu(high, rows[:, members:])
    half = planes_dev * members_dev
    gain = (total[:half] + total[half:] + extra) * scale
    for plane in range(planes_dev):
        gain_ref[plane] = gain[plane * members_dev : (plane + 1) * members_dev]


def update_kernel(*refs, groups, members, planes_dev):
    states, gain_ref, out_ref = refs[:-2], refs[-2], refs[-1]
    blocks, rows, width = states[0].shape
    members_dev = rows // planes_dev
    member_count = jnp.float32(members)
    for plane in range(planes_dev):
        high, low = halves(gain_ref[plane])
        both = jnp.concatenate([high, low], axis=0)
        top = plane * members_dev
        for block in range(blocks):
            parts = []
            for group in groups:
                part = states[group[0]][block, top : top + members_dev, :]
                for other in group[1:]:
                    part = part + states[other][block, top : top + members_dev, :]
                parts.append(part)
            values = jnp.concatenate(parts, axis=0)
            anom = values - jnp.sum(values, axis=0, keepdims=True) / member_count
            anom_hi, anom_lo = halves(anom)
            moved = mxu(both, anom_hi)
            moved = moved[:members_dev] + moved[members_dev:] + mxu(high, anom_lo)
            out_ref[:, plane, block * width : (block + 1) * width] = parts[0] + moved


def on_core(kernel, shape, flops, moved, scratch=(), name=None):
    return pl.pallas_call(
        kernel,
        out_shape=jax.ShapeDtypeStruct(shape, jnp.float32),
        scratch_shapes=list(scratch),
        cost_estimate=pl.CostEstimate(flops=flops, bytes_accessed=moved, transcendentals=0),
        name=name,
    )


def replicated(ensemble, forcing, obs_cell, obs_value, obs_var, obs_noise):
    members_dev, planes_dev, plane_cells = ensemble.shape
    obs_dev = obs_cell.shape[0]
    slabs = lax.axis_size("space")
    mem_count = lax.axis_size("mem")
    members = members_dev * mem_count
    reach_slabs = min(8, slabs // 4)
    width = plane_cells // slabs
    state_rows = planes_dev * members_dev
    sent_rows = round_up(state_rows + planes_dev, SUBLANES)
    state_bytes = 4 * ensemble.size

    packed = on_core(
        pack_kernel, (slabs, sent_rows, width), ensemble.size, 2 * state_bytes, name="pack"
    )(ensemble, forcing)
    columns = lax.all_to_all(packed, "space", 0, 0, tiled=True)
    ahead = on_core(
        functools.partial(forecast_kernel, planes_dev=planes_dev, members_dev=members_dev),
        (slabs, state_rows, width),
        24 * ensemble.size,
        2 * state_bytes,
        name="forecast",
    )(columns)
    states = lax.all_to_all(ahead, "space", 0, 0, tiled=True)

    observed = on_core(
        functools.partial(
            observe_kernel,
            planes_dev=planes_dev,
            members_dev=members_dev,
            plane_cells=plane_cells,
        ),
        (members_dev, obs_dev),
        6 * ensemble.size * obs_dev,
        state_bytes,
        name="observe",
    )(states, obs_cell[None, :])

    pieces = [observed] + [flipped(observed, "mem", n) for n in range(1, mem_count)]
    one_away = flipped(states, "mem", 1)
    two_away = flipped(states, "mem", 2)
    inner = lax.ppermute(states, "mem", [(1, 2), (2, 1)])
    outer = lax.ppermute(two_away, "mem", [(2, 3), (1, 0)])

    wanted = obs_value + jnp.sqrt(obs_var) * obs_noise
    place = (obs_cell // plane_cells).astype(jnp.float32)
    side = jnp.concatenate(
        [obs_var[None], place[None], jnp.zeros((SUBLANES - 2, obs_dev), jnp.float32)]
    )
    block = jnp.concatenate(pieces + [wanted, side], axis=0)
    near = [flipped(block, "space", n) if n else block for n in range(0, slabs, 2)]
    gathered = []
    for n in range(slabs // 2):
        gathered += [near[n], flipped(near[n], "space", 1)]

    pair = 2
    tiles = slabs // pair
    near_tiles = min(tiles, 1 + 2 * (-(-reach_slabs // pair)))
    tile = pair * obs_dev
    count = slabs * obs_dev
    low_type = jnp.bfloat16
    gain = on_core(
        functools.partial(
            solve_kernel,
            members=members,
            members_dev=members_dev,
            planes_dev=planes_dev,
            pair=pair,
            reach_slabs=reach_slabs,
        ),
        (planes_dev, members_dev, members),
        6 * count * count * (members + 2 * ITERS * members_dev),
        4 * count * (members + members_dev),
        [
            pltpu.VMEM((slabs, 3 * members, obs_dev), low_type),
            pltpu.VMEM((slabs, obs_dev, 2 * members), low_type),
            pltpu.VMEM((slabs, SUBLANES, obs_dev), jnp.float32),
            pltpu.VMEM((tiles, near_tiles * tile, tile), low_type),
            pltpu.VMEM((tiles, near_tiles * tile, tile), low_type),
            pltpu.VMEM((slabs, members_dev, obs_dev), jnp.float32),
            pltpu.VMEM((slabs, members_dev, obs_dev), jnp.float32),
            pltpu.VMEM((slabs, members_dev, obs_dev), jnp.float32),
            pltpu.VMEM((2 * members_dev, count), low_type),
        ],
        name="solve",
    )(*gathered)

    return on_core(
        functools.partial(
            update_kernel,
            groups=((0,), (1,), (2,), (3, 4)),
            members=members,
            planes_dev=planes_dev,
        ),
        ensemble.shape,
        6 * ensemble.size * members,
        6 * state_bytes,
        name="update",
    )(states, one_away, two_away, inner, outer, gain)


def shards(ensemble, forcing, obs_cell, obs_value, obs_var, obs_noise):
    args = (ensemble, forcing, obs_cell, obs_value, obs_var, obs_noise)
    members_dev, planes_dev, plane_cells = ensemble.shape
    slabs, groups, obs_dev = (lax.axis_size("space"), lax.axis_size("mem"), obs_cell.shape[0])
    aligned = (
        obs_dev % LANES == 0
        and plane_cells % (slabs * LANES) == 0
        and members_dev % SUBLANES == 0
        and (members_dev * groups) % LANES == 0
    )
    small = 4 * (slabs * obs_dev) ** 2 <= 2**24
    paired = slabs & (slabs - 1) == 0 and slabs >= 4
    if aligned and small and paired and groups == 4:
        return replicated(*args)
    return banded(*args)


def solution(mesh):
    placed = (
        P("mem", "space", None),
        P("space", None),
        P("space"),
        P("space"),
        P("space"),
        P("mem", "space"),
    )
    return jax.shard_map(
        shards, mesh=mesh, in_specs=placed, out_specs=P("mem", "space", None), check_vma=False
    )
```

```python
import functools

import jax
import jax.numpy as jnp
from jax import lax
from jax.experimental import pallas as pl
from jax.experimental.pallas import tpu as pltpu
from jax.sharding import PartitionSpec as P


FSTEPS = 4
ITERS = 6
LANES = 128
SUBLANES = 8

time_step = 0.05
highest = lax.Precision.HIGHEST


def from_behind(value, axis, steps):
    count = lax.axis_size(axis)
    pairs = [(source, (source + steps) % count) for source in range(count)]
    return lax.ppermute(value, axis, pairs)


def flipped(value, axis, mask):
    count = lax.axis_size(axis)
    return lax.ppermute(value, axis, [(i, i ^ mask) for i in range(count)])


def padded_2(x, sides, width):
    for axis, dim in sides:
        size, length = (lax.axis_size(axis), x.shape[dim])
        up = [(i, (i + 1) % size) for i in range(size)]
        down = [(j, i) for i, j in up]
        last = lax.slice_in_dim(x, length - width, length, axis=dim)
        initial = lax.slice_in_dim(x, 0, width, axis=dim)
        before = lax.ppermute(last, axis, up)
        after = lax.ppermute(initial, axis, down)
        x = jnp.concatenate([before, x, after], axis=dim)
    return x


def taper_of(planes_a, planes_b, planes_all, reach_planes):
    spread = jnp.abs(planes_a[:, None] - planes_b[None, :])
    spread = jnp.minimum(spread, planes_all - spread)
    return jnp.maximum(0.0, 1.0 - spread.astype(jnp.float32) / reach_planes)


def collect_band(values, along, reach_slabs):
    pieces = []
    for offset in range(-reach_slabs, reach_slabs + 1):
        if offset == 0:
            pieces.append(values)
        else:
            pieces.append(from_behind(values, "space", -offset))
    return jnp.concatenate(pieces, axis=along)


def banded(ensemble, forcing, obs_cell, obs_value, obs_var, obs_noise):
    members_dev, planes_dev, plane_cells = ensemble.shape
    obs_dev = obs_cell.shape[0]
    space_count = lax.axis_size("space")
    mem_count = lax.axis_size("mem")
    space_index = lax.axis_index("space")
    mem_index = lax.axis_index("mem")
    members = members_dev * mem_count
    planes_all = planes_dev * space_count
    reach_slabs = min(8, space_count // 4)
    reach_planes = planes_dev * reach_slabs
    band_width = reach_slabs * obs_dev
    states = ensemble
    for _ in range(FSTEPS):
        padded = padded_2(states, (("space", 1),), 2)
        forward_one = padded[:, 3 : 3 + planes_dev]
        back_one = padded[:, 1 : 1 + planes_dev]
        back_two = padded[:, 0:planes_dev]
        states = states + time_step * ((forward_one - back_two) * back_one - states + forcing)
    slab_cells = planes_dev * plane_cells
    local_cells = obs_cell - space_index * slab_cells
    observed = jnp.take(states.reshape(members_dev, slab_cells), local_cells, axis=1)
    own_planes = obs_cell // plane_cells
    own_rows = lax.all_gather(observed, "mem", axis=0, tiled=True)
    own_mean = jnp.sum(own_rows, axis=0) / members
    own_anom = own_rows - own_mean
    stacked = jnp.concatenate([own_anom, own_planes.astype(jnp.float32)[None, :]], axis=0)
    band = collect_band(stacked, 1, reach_slabs)
    context_anom = band[:members]
    context_planes = band[members].astype(jnp.int32)
    context_count = context_anom.shape[1]
    taper_block = taper_of(own_planes, context_planes, planes_all, reach_planes)
    gram_block = jnp.dot(own_anom.T, context_anom, precision=highest) / (members - 1)
    diagonal = jnp.arange(context_count)[None, :] == (band_width + jnp.arange(obs_dev))[:, None]
    covariance = taper_block * gram_block + jnp.where(diagonal, obs_var[:, None], 0.0)
    row_max = jnp.max(jnp.sum(jnp.abs(covariance), axis=1))
    var_min = jnp.min(obs_var)
    both = lax.pmax((row_max, -var_min), "space")
    upper_bound = both[0]
    lower_bound = -both[1]
    mean_rhs = obs_value - own_mean
    member_anom = lax.dynamic_slice_in_dim(own_anom, mem_index * members_dev, members_dev, 0)
    anom_rhs = (jnp.sqrt(obs_var)[None, :] * obs_noise - member_anom).T
    center = (upper_bound + lower_bound) / 2.0
    radius = (upper_bound - lower_bound) / 2.0
    sigma_ratio = center / radius
    rho_now = 1.0 / sigma_ratio
    resid_anom, resid_mean = (anom_rhs, mean_rhs)
    dir_anom, dir_mean = (anom_rhs / center, mean_rhs / center)
    anom_weight = jnp.zeros_like(anom_rhs)
    mean_weight = jnp.zeros_like(mean_rhs)
    for iteration in range(ITERS):
        anom_weight = anom_weight + dir_anom
        mean_weight = mean_weight + dir_mean
        if iteration < ITERS - 1:
            joined = jnp.concatenate([dir_anom, dir_mean[:, None]], axis=1)
            band_dirs = collect_band(joined, 0, reach_slabs)
            image = jnp.dot(covariance, band_dirs, precision=highest)
            image_anom = image[:, :-1]
            image_mean = image[:, -1]
            resid_anom = resid_anom - image_anom
            resid_mean = resid_mean - image_mean
            rho_next = 1.0 / (2.0 * sigma_ratio - rho_now)
            dir_anom = rho_next * rho_now * dir_anom + 2.0 * rho_next / radius * resid_anom
            dir_mean = rho_next * rho_now * dir_mean + 2.0 * rho_next / radius * resid_mean
            rho_now = rho_next
    weight = anom_weight + mean_weight[:, None]
    owned_cells = lax.all_to_all(states, "mem", split_axis=2, concat_axis=0, tiled=True)
    weight_rows = lax.all_gather(weight, "mem", axis=1, tiled=True)
    weight_context = collect_band(weight_rows, 0, reach_slabs)
    own_plane_ids = space_index * planes_dev + jnp.arange(planes_dev, dtype=jnp.int32)
    plane_taper = taper_of(own_plane_ids, context_planes, planes_all, reach_planes)

    def plane_gain(taper_row):
        return jnp.dot(context_anom * taper_row[None, :], weight_context, precision=highest)

    gain_blocks = lax.map(plane_gain, plane_taper)
    state_mean = jnp.sum(owned_cells, axis=0) / members
    state_anom = owned_cells - state_mean
    update = jnp.einsum("jxp,xjk->kxp", state_anom, gain_blocks, precision=highest) / (members - 1)
    analysis = owned_cells + update
    return lax.all_to_all(analysis, "mem", split_axis=0, concat_axis=2, tiled=True)


def halves(x):
    high = x.astype(jnp.bfloat16)
    low = (x - high.astype(jnp.float32)).astype(jnp.bfloat16)
    return high, low


def mxu(a, b):
    return jnp.dot(a, b, preferred_element_type=jnp.float32)


def round_up(value, unit):
    return -(-value // unit) * unit


def pack_kernel(ens_hbm, forcing_hbm, cell_ref, value_ref, var_ref, noise_ref, *rest, slabs):
    give_ref, keep_ref, side_ref, local_ref, ens, forcing, sems = rest
    members_dev, planes_dev, cells = ens.shape
    blocks, rows, width = give_ref.shape
    state_rows = planes_dev * members_dev
    me = lax.axis_index("space")
    smalls = pltpu.make_async_copy(forcing_hbm, forcing, sems.at[0])
    smalls.start()
    copies = []
    for _ in range(1):
        copy = pltpu.make_async_copy(ens_hbm, ens, sems.at[1])
        copy.start()
        copies.append(copy)
    local_ref[...] = cell_ref[...] - me * (planes_dev * cells)
    side_ref[:members_dev] = value_ref[...] + jnp.sqrt(var_ref[...]) * noise_ref[...]
    base = me * planes_dev
    place = jnp.zeros(cell_ref.shape, jnp.float32) + base.astype(jnp.float32)
    for plane in range(1, planes_dev):
        place = place + jnp.where(local_ref[...] >= plane * cells, 1.0, 0.0)
    fill = jnp.zeros((SUBLANES - 2, cell_ref.shape[1]), jnp.float32)
    side_ref[members_dev:] = jnp.concatenate([var_ref[...], place, fill], axis=0)
    smalls.wait()
    for copy in copies:
        copy.wait()
    tail = jnp.zeros((rows - state_rows - planes_dev, width), jnp.float32)
    for hop in range(blocks):
        for ref, flip in ((give_ref, 1), (keep_ref, 0)):
            first = jnp.bitwise_xor(me, 2 * hop + flip) * width
            span = pl.ds(pl.multiple_of(first, width), width)
            for plane in range(planes_dev):
                top = plane * members_dev
                ref[hop, top : top + members_dev, :] = ens[:, plane, span]
            ref[hop, state_rows:, :] = jnp.concatenate([forcing[:, span], tail], axis=0)


def join_kernel(keep_ref, got_ref, *outs):
    skip = keep_ref.shape[0] - len(outs)
    for hop, out in enumerate(outs):
        out[0] = keep_ref[hop + skip]
        out[1] = got_ref[hop + skip]


def forecast_kernel(*refs, planes_dev, members_dev, slabs):
    keep_ref, got_ref, others = refs[0], refs[1], refs[2 : 1 + slabs // 2]
    own_ref, cross_ref, grid_ref = refs[1 + slabs // 2 :]
    width = own_ref.shape[2]
    state_rows = planes_dev * members_dev
    count = slabs * planes_dev
    me = lax.axis_index("space")
    grid_ref[me] = keep_ref[0]
    grid_ref[jnp.bitwise_xor(me, 1)] = got_ref[0]
    for hop, other in enumerate(others):
        for flip in range(2):
            grid_ref[jnp.bitwise_xor(me, 2 * hop + 2 + flip)] = other[flip]
    for lane in range(0, width, LANES):
        lanes = slice(lane, lane + LANES)
        drive = []
        for plane in range(count):
            row = state_rows + plane % planes_dev
            drive.append(grid_ref[plane // planes_dev, row : row + 1, lanes])
        for member in range(0, members_dev, SUBLANES):
            column = []
            for plane in range(count):
                top = (plane % planes_dev) * members_dev + member
                column.append(grid_ref[plane // planes_dev, top : top + SUBLANES, lanes])
            for _ in range(FSTEPS):
                column = [
                    column[n]
                    + time_step
                    * (
                        (column[(n + 1) % count] - column[n - 2]) * column[n - 1]
                        - column[n]
                        + drive[n]
                    )
                    for n in range(count)
                ]
            for plane in range(count):
                top = (plane % planes_dev) * members_dev + member
                grid_ref[plane // planes_dev, top : top + SUBLANES, lanes] = column[plane]
    for hop in range(slabs // 2):
        own_ref[hop] = grid_ref[jnp.bitwise_xor(me, 2 * hop), :state_rows]
        cross_ref[hop] = grid_ref[jnp.bitwise_xor(me, 2 * hop + 1), :state_rows]


def observe_kernel(*refs, planes_dev, members_dev, plane_cells):
    pieces, (local_ref, out_ref, rest_ref, whole_ref) = refs[:-4], refs[-4:]
    width = rest_ref.shape[2]
    obs_dev = local_ref.shape[1]
    me = lax.axis_index("space")
    local = local_ref[...]
    total = jnp.zeros((3 * members_dev, obs_dev), jnp.float32)
    for hop, piece in enumerate(pieces):
        for flip in range(2):
            block = jnp.bitwise_xor(me, 2 * hop + flip)
            if hop:
                rest_ref[2 * hop - 2 + flip] = piece[flip]
            whole_ref[2 * hop + flip] = piece[flip]
            for plane in range(planes_dev):
                base = plane * plane_cells + block * width
                index = lax.broadcasted_iota(jnp.int32, (width, obs_dev), 0)
                pick = (index == local - base).astype(jnp.float32).astype(jnp.bfloat16)
                top = plane * members_dev
                values = piece[flip, top : top + members_dev, :]
                high = values.astype(jnp.bfloat16)
                middle, low = halves(values - high.astype(jnp.float32))
                total += mxu(jnp.concatenate([high, middle, low], axis=0), pick)
    out_ref[...] = (
        total[:members_dev]
        + total[members_dev : 2 * members_dev]
        + total[2 * members_dev :]
    )


def stack_kernel(*refs):
    out_ref = refs[-1]
    row = 0
    for ref in refs[:-1]:
        out_ref[row : row + ref.shape[0], :] = ref[...]
        row += ref.shape[0]


def solve_kernel(*refs, members, members_dev, planes_dev, pair, reach_slabs):
    slabs = len(refs) - 10
    ins, gain_ref = refs[:slabs], refs[slabs]
    anom_ref, flip_ref, side_ref, cov_hi, cov_lo, dir_ref, res_ref, sol_ref, split_ref = refs[
        slabs + 1 :
    ]
    obs_dev = ins[0].shape[1]
    planes_all = planes_dev * slabs
    reach_planes = planes_dev * reach_slabs
    me = lax.axis_index("space")
    member_count = jnp.float32(members)

    for offset in range(slabs):
        slab = jnp.bitwise_xor(me, offset)
        block = ins[offset][...]
        observed = block[:members]
        mean = jnp.sum(observed, axis=0, keepdims=True) / member_count
        anom = observed - mean
        high, low = halves(anom)
        anom_ref[slab, :members] = high
        anom_ref[slab, members : 2 * members] = high
        anom_ref[slab, 2 * members :] = low
        turned = anom.T
        turned_hi, turned_lo = halves(turned)
        flip_ref[slab, :, :members] = turned_hi
        flip_ref[slab, :, members:] = turned_lo
        res_ref[slab] = block[members : members + members_dev] - observed[:members_dev]
        side_ref[slab] = block[members + members_dev : members + members_dev + SUBLANES]

    lower = None
    variances, places, columns = [], [], []
    for slab in range(slabs):
        side = side_ref[slab]
        variances.append(side[0:1])
        places.append(side[1:2])
        columns.append(side.T[:, 1:2])
    var_row = jnp.concatenate(variances, axis=1)
    place_row = jnp.concatenate(places, axis=1)
    lower = jnp.min(var_row, axis=1, keepdims=True)

    tile = pair * obs_dev
    tiles = slabs // pair
    reach_tiles = -(-reach_slabs // pair)
    near = {}
    for right in range(tiles):
        near[right] = sorted({(right + step) % tiles for step in range(-reach_tiles, reach_tiles + 1)})
    scale = jnp.float32(1.0 / (members - 1))
    upper = None
    for right in range(tiles):
        span = slice(right * tile, (right + 1) * tile)
        tops = jnp.concatenate(
            [anom_ref[right * pair + n, : 2 * members] for n in range(pair)], axis=1
        )
        lows = jnp.concatenate(
            [anom_ref[right * pair + n, 2 * members :] for n in range(pair)], axis=1
        )
        along = place_row[:, span]
        sums = None
        for order, left in enumerate(near[right]):
            for part in range(pair):
                slab = left * pair + part
                rows = flip_ref[slab]
                gram = mxu(rows, tops) + mxu(rows[:, :members], lows)
                spread = jnp.abs(columns[slab] - along)
                spread = jnp.minimum(spread, planes_all - spread)
                taper = jnp.maximum(0.0, 1.0 - spread / reach_planes)
                cov = taper * (gram * scale)
                if left == right:
                    below = lax.broadcasted_iota(jnp.int32, (obs_dev, tile), 0) + part * obs_dev
                    across = lax.broadcasted_iota(jnp.int32, (obs_dev, tile), 1)
                    cov = cov + jnp.where(below == across, var_row[:, span], 0.0)
                size = jnp.sum(jnp.abs(cov), axis=0, keepdims=True)
                sums = size if sums is None else sums + size
                high, low = halves(cov)
                top = (order * pair + part) * obs_dev
                cov_hi[right, top : top + obs_dev, :] = high
                cov_lo[right, top : top + obs_dev, :] = low
        biggest = jnp.max(sums, axis=1, keepdims=True)
        upper = biggest if upper is None else jnp.maximum(upper, biggest)

    center = (upper + lower) / 2.0
    radius = (upper - lower) / 2.0
    sigma_ratio = center / radius
    rho_now = 1.0 / sigma_ratio
    for slab in range(slabs):
        span = slice(slab * obs_dev, (slab + 1) * obs_dev)
        start = res_ref[slab] / center
        dir_ref[slab] = start
        sol_ref[slab] = start
        high, low = halves(start)
        split_ref[:members_dev, span] = high
        split_ref[members_dev:, span] = low
    for iteration in range(ITERS - 1):
        rho_next = 1.0 / (2.0 * sigma_ratio - rho_now)
        keep = rho_next * rho_now
        take = 2.0 * rho_next / radius
        images = []
        for right in range(tiles):
            lefts = jnp.concatenate(
                [split_ref[:, left * tile : (left + 1) * tile] for left in near[right]], axis=1
            )
            both = mxu(lefts, cov_hi[right])
            images.append(
                both[:members_dev]
                + both[members_dev:]
                + mxu(lefts[:members_dev], cov_lo[right])
            )
        for slab in range(slabs):
            span = slice(slab * obs_dev, (slab + 1) * obs_dev)
            part = slab % pair
            image = images[slab // pair][:, part * obs_dev : (part + 1) * obs_dev]
            residual = res_ref[slab] - image
            res_ref[slab] = residual
            ahead = keep * dir_ref[slab] + take * residual
            dir_ref[slab] = ahead
            sol_ref[slab] += ahead
            if iteration < ITERS - 2:
                high, low = halves(ahead)
                split_ref[:members_dev, span] = high
                split_ref[members_dev:, span] = low
        rho_now = rho_next

    total = jnp.zeros((2 * planes_dev * members_dev, members), jnp.float32)
    extra = jnp.zeros((planes_dev * members_dev, members), jnp.float32)
    for slab in range(slabs):
        weight = sol_ref[slab]
        tapered = []
        for plane in range(planes_dev):
            own = (me * planes_dev + plane).astype(jnp.float32)
            spread = jnp.abs(own - place_row[:, slab * obs_dev : (slab + 1) * obs_dev])
            spread = jnp.minimum(spread, planes_all - spread)
            tapered.append(weight * jnp.maximum(0.0, 1.0 - spread / reach_planes))
        high, low = halves(jnp.concatenate(tapered, axis=0))
        rows = flip_ref[slab]
        total += mxu(jnp.concatenate([high, low], axis=0), rows[:, :members])
        extra += mxu(high, rows[:, members:])
    half = planes_dev * members_dev
    gain = (total[:half] + total[half:] + extra) * scale
    for plane in range(planes_dev):
        gain_ref[plane] = gain[plane * members_dev : (plane + 1) * members_dev]


def update_kernel(
    whole_ref, home_ref, rest_ref, far_ref, inner_ref, outer_ref, gain_ref, out_ref, *, members, planes_dev
):
    blocks, rows, width = whole_ref.shape
    members_dev = rows // planes_dev
    split = home_ref.shape[0]
    member_count = jnp.float32(members)
    me = lax.axis_index("space")
    for plane in range(planes_dev):
        high, low = halves(gain_ref[plane])
        both = jnp.concatenate([high, low], axis=0)
        span = slice(plane * members_dev, (plane + 1) * members_dev)
        for block in range(blocks):
            own = whole_ref[block, span, :]
            one = home_ref[block, span, :] if block < split else rest_ref[block - split, span, :]
            last = inner_ref[block, span, :] + outer_ref[block, span, :]
            values = jnp.concatenate([own, one, far_ref[block, span, :], last], axis=0)
            anom = values - jnp.sum(values, axis=0, keepdims=True) / member_count
            anom_hi, anom_lo = halves(anom)
            change = mxu(both, anom_hi)
            change = change[:members_dev] + change[members_dev:] + mxu(high, anom_lo)
            start = jnp.bitwise_xor(me, block) * width
            out_ref[:, plane, pl.ds(pl.multiple_of(start, width), width)] = own + change


def on_core(kernel, shapes, flops, moved, scratch=(), room=8, in_specs=None):
    single = not isinstance(shapes, list)
    many = [shapes] if single else shapes
    out = [x if hasattr(x, "dtype") else jax.ShapeDtypeStruct(x, jnp.float32) for x in many]
    extra = {} if in_specs is None else {"in_specs": in_specs}
    return pl.pallas_call(
        kernel,
        compiler_params=pltpu.CompilerParams(vmem_limit_bytes=room * 2**20),
        out_shape=out[0] if single else out,
        scratch_shapes=list(scratch),
        cost_estimate=pl.CostEstimate(flops=flops, bytes_accessed=moved, transcendentals=0),
        **extra,
    )


def replicated(ensemble, forcing, obs_cell, obs_value, obs_var, obs_noise):
    members_dev, planes_dev, plane_cells = ensemble.shape
    obs_dev = obs_cell.shape[0]
    slabs = lax.axis_size("space")
    mem_count = lax.axis_size("mem")
    members = members_dev * mem_count
    reach_slabs = min(8, slabs // 4)
    width = plane_cells // slabs
    state_rows = planes_dev * members_dev
    sent_rows = round_up(state_rows + planes_dev, SUBLANES)
    state_bytes = 4 * ensemble.size
    hops = slabs // 2
    sizes = dict(planes_dev=planes_dev, members_dev=members_dev)
    in_hbm = pl.BlockSpec(memory_space=pltpu.HBM)
    in_vmem = pl.BlockSpec(memory_space=pltpu.VMEM)

    give, keep, side, local = on_core(
        functools.partial(pack_kernel, slabs=slabs),
        [
            (hops, sent_rows, width),
            (hops, sent_rows, width),
            (members_dev + SUBLANES, obs_dev),
            jax.ShapeDtypeStruct((1, obs_dev), jnp.int32),
        ],
        ensemble.size,
        2 * state_bytes,
        scratch=[
            pltpu.VMEM(ensemble.shape, jnp.float32),
            pltpu.VMEM(forcing.shape, jnp.float32),
            pltpu.SemaphoreType.DMA((2,)),
        ],
        in_specs=[in_hbm, in_hbm] + [in_vmem] * 4,
    )(ensemble, forcing, obs_cell[None], obs_value[None], obs_var[None], obs_noise)
    got = flipped(give, "space", 1)
    sent = on_core(join_kernel, [(2, sent_rows, width)] * (hops - 1), 1, 2 * state_bytes)(keep, got)
    come = [flipped(sent[n - 1], "space", 2 * n) for n in range(1, hops)]
    own, cross = on_core(
        functools.partial(forecast_kernel, slabs=slabs, **sizes),
        [(hops, state_rows, width)] * 2,
        24 * ensemble.size,
        2 * state_bytes,
        scratch=[pltpu.VMEM((slabs, sent_rows, width), jnp.float32)],
    )(keep, got, *come)

    crossed = flipped(cross, "space", 1)
    back = on_core(join_kernel, [(2, state_rows, width)] * hops, 1, 2 * state_bytes)(own, crossed)
    home = back[0]
    pieces = [home] + [flipped(back[n], "space", 2 * n) for n in range(1, hops)]
    home_two = flipped(home, "mem", 2)
    home_one = flipped(home, "mem", 1)
    observed, rest, whole = on_core(
        functools.partial(observe_kernel, plane_cells=plane_cells, **sizes),
        [
            (members_dev, obs_dev),
            (slabs - 2, state_rows, width),
            (slabs, state_rows, width),
        ],
        6 * ensemble.size * obs_dev,
        state_bytes,
    )(*pieces, local)

    seen = [observed] + [flipped(observed, "mem", n) for n in range(1, mem_count)]
    rest_two = flipped(rest, "mem", 2)
    rest_one = flipped(rest, "mem", 1)
    block = on_core(
        stack_kernel, (members + members_dev + SUBLANES, obs_dev), 1, 8 * members * obs_dev
    )(*seen, side)
    near = [flipped(block, "space", n) if n else block for n in range(0, slabs, 2)]
    gathered = []
    for n in range(slabs // 2):
        gathered += [near[n], flipped(near[n], "space", 1)]

    whole, gathered = lax.optimization_barrier((whole, gathered))
    inner = lax.ppermute(whole, "mem", [(1, 2), (2, 1)])

    pair = 2
    tiles = slabs // pair
    near_tiles = min(tiles, 1 + 2 * (-(-reach_slabs // pair)))
    tile = pair * obs_dev
    count = slabs * obs_dev
    low_type = jnp.bfloat16
    gain = on_core(
        functools.partial(
            solve_kernel, members=members, pair=pair, reach_slabs=reach_slabs, **sizes
        ),
        (planes_dev, members_dev, members),
        6 * count * count * (members + 2 * ITERS * members_dev),
        4 * count * (members + members_dev),
        [
            pltpu.VMEM((slabs, 3 * members, obs_dev), low_type),
            pltpu.VMEM((slabs, obs_dev, 2 * members), low_type),
            pltpu.VMEM((slabs, SUBLANES, obs_dev), jnp.float32),
            pltpu.VMEM((tiles, near_tiles * tile, tile), low_type),
            pltpu.VMEM((tiles, near_tiles * tile, tile), low_type),
            pltpu.VMEM((slabs, members_dev, obs_dev), jnp.float32),
            pltpu.VMEM((slabs, members_dev, obs_dev), jnp.float32),
            pltpu.VMEM((slabs, members_dev, obs_dev), jnp.float32),
            pltpu.VMEM((2 * members_dev, count), low_type),
        ],
        room=20,
    )(*gathered)

    home_two, rest_two, gain = lax.optimization_barrier((home_two, rest_two, gain))
    far = on_core(stack_kernel, (slabs, state_rows, width), 1, 2 * state_bytes)(home_two, rest_two)
    outer = lax.ppermute(far, "mem", [(2, 3), (1, 0)])
    return on_core(
        functools.partial(
            update_kernel,
            members=members,
            planes_dev=planes_dev,
        ),
        ensemble.shape,
        6 * ensemble.size * members,
        6 * state_bytes,
        room=12,
    )(whole, home_one, rest_one, far, inner, outer, gain)


def shards(ensemble, forcing, obs_cell, obs_value, obs_var, obs_noise):
    args = (ensemble, forcing, obs_cell, obs_value, obs_var, obs_noise)
    members_dev, _, plane_cells = ensemble.shape
    slabs, groups, obs_dev = (lax.axis_size("space"), lax.axis_size("mem"), obs_cell.shape[0])
    aligned = (
        obs_dev % LANES == 0
        and plane_cells % (slabs * LANES) == 0
        and members_dev % SUBLANES == 0
        and (members_dev * groups) % LANES == 0
    )
    small = 4 * (slabs * obs_dev) ** 2 <= 2**24
    paired = slabs & (slabs - 1) == 0 and slabs >= 4
    if aligned and small and paired and groups == 4:
        return replicated(*args)
    return banded(*args)


def solution(mesh):
    placed = (
        P("mem", "space", None),
        P("space", None),
        P("space"),
        P("space"),
        P("space"),
        P("mem", "space"),
    )
    return jax.shard_map(
        shards, mesh=mesh, in_specs=placed, out_specs=P("mem", "space", None), check_vma=False
    )
```

```python
import functools

import jax
import jax.numpy as jnp
from jax import lax
from jax.experimental import pallas as pl
from jax.experimental.pallas import tpu as pltpu
from jax.sharding import PartitionSpec as P


FSTEPS = 4
ITERS = 6
LANES = 128
SUBLANES = 8

time_step = 0.05
highest = lax.Precision.HIGHEST


def from_behind(value, axis, steps):
    count = lax.axis_size(axis)
    pairs = [(source, (source + steps) % count) for source in range(count)]
    return lax.ppermute(value, axis, pairs)


def flipped(value, axis, mask):
    count = lax.axis_size(axis)
    return lax.ppermute(value, axis, [(i, i ^ mask) for i in range(count)])


def padded_2(x, sides, width):
    for axis, dim in sides:
        size, length = (lax.axis_size(axis), x.shape[dim])
        up = [(i, (i + 1) % size) for i in range(size)]
        down = [(j, i) for i, j in up]
        last = lax.slice_in_dim(x, length - width, length, axis=dim)
        initial = lax.slice_in_dim(x, 0, width, axis=dim)
        before = lax.ppermute(last, axis, up)
        after = lax.ppermute(initial, axis, down)
        x = jnp.concatenate([before, x, after], axis=dim)
    return x


def taper_of(planes_a, planes_b, planes_all, reach_planes):
    spread = jnp.abs(planes_a[:, None] - planes_b[None, :])
    spread = jnp.minimum(spread, planes_all - spread)
    return jnp.maximum(0.0, 1.0 - spread.astype(jnp.float32) / reach_planes)


def collect_band(values, along, reach_slabs):
    pieces = []
    for offset in range(-reach_slabs, reach_slabs + 1):
        if offset == 0:
            pieces.append(values)
        else:
            pieces.append(from_behind(values, "space", -offset))
    return jnp.concatenate(pieces, axis=along)


def banded(ensemble, forcing, obs_cell, obs_value, obs_var, obs_noise):
    members_dev, planes_dev, plane_cells = ensemble.shape
    obs_dev = obs_cell.shape[0]
    space_count = lax.axis_size("space")
    mem_count = lax.axis_size("mem")
    space_index = lax.axis_index("space")
    mem_index = lax.axis_index("mem")
    members = members_dev * mem_count
    planes_all = planes_dev * space_count
    reach_slabs = min(8, space_count // 4)
    reach_planes = planes_dev * reach_slabs
    band_width = reach_slabs * obs_dev
    states = ensemble
    for _ in range(FSTEPS):
        padded = padded_2(states, (("space", 1),), 2)
        forward_one = padded[:, 3 : 3 + planes_dev]
        back_one = padded[:, 1 : 1 + planes_dev]
        back_two = padded[:, 0:planes_dev]
        states = states + time_step * ((forward_one - back_two) * back_one - states + forcing)
    slab_cells = planes_dev * plane_cells
    local_cells = obs_cell - space_index * slab_cells
    observed = jnp.take(states.reshape(members_dev, slab_cells), local_cells, axis=1)
    own_planes = obs_cell // plane_cells
    own_rows = lax.all_gather(observed, "mem", axis=0, tiled=True)
    own_mean = jnp.sum(own_rows, axis=0) / members
    own_anom = own_rows - own_mean
    stacked = jnp.concatenate([own_anom, own_planes.astype(jnp.float32)[None, :]], axis=0)
    band = collect_band(stacked, 1, reach_slabs)
    context_anom = band[:members]
    context_planes = band[members].astype(jnp.int32)
    context_count = context_anom.shape[1]
    taper_block = taper_of(own_planes, context_planes, planes_all, reach_planes)
    gram_block = jnp.dot(own_anom.T, context_anom, precision=highest) / (members - 1)
    diagonal = jnp.arange(context_count)[None, :] == (band_width + jnp.arange(obs_dev))[:, None]
    covariance = taper_block * gram_block + jnp.where(diagonal, obs_var[:, None], 0.0)
    row_max = jnp.max(jnp.sum(jnp.abs(covariance), axis=1))
    var_min = jnp.min(obs_var)
    both = lax.pmax((row_max, -var_min), "space")
    upper_bound = both[0]
    lower_bound = -both[1]
    mean_rhs = obs_value - own_mean
    member_anom = lax.dynamic_slice_in_dim(own_anom, mem_index * members_dev, members_dev, 0)
    anom_rhs = (jnp.sqrt(obs_var)[None, :] * obs_noise - member_anom).T
    center = (upper_bound + lower_bound) / 2.0
    radius = (upper_bound - lower_bound) / 2.0
    sigma_ratio = center / radius
    rho_now = 1.0 / sigma_ratio
    resid_anom, resid_mean = (anom_rhs, mean_rhs)
    dir_anom, dir_mean = (anom_rhs / center, mean_rhs / center)
    anom_weight = jnp.zeros_like(anom_rhs)
    mean_weight = jnp.zeros_like(mean_rhs)
    for iteration in range(ITERS):
        anom_weight = anom_weight + dir_anom
        mean_weight = mean_weight + dir_mean
        if iteration < ITERS - 1:
            joined = jnp.concatenate([dir_anom, dir_mean[:, None]], axis=1)
            band_dirs = collect_band(joined, 0, reach_slabs)
            image = jnp.dot(covariance, band_dirs, precision=highest)
            image_anom = image[:, :-1]
            image_mean = image[:, -1]
            resid_anom = resid_anom - image_anom
            resid_mean = resid_mean - image_mean
            rho_next = 1.0 / (2.0 * sigma_ratio - rho_now)
            dir_anom = rho_next * rho_now * dir_anom + 2.0 * rho_next / radius * resid_anom
            dir_mean = rho_next * rho_now * dir_mean + 2.0 * rho_next / radius * resid_mean
            rho_now = rho_next
    weight = anom_weight + mean_weight[:, None]
    owned_cells = lax.all_to_all(states, "mem", split_axis=2, concat_axis=0, tiled=True)
    weight_rows = lax.all_gather(weight, "mem", axis=1, tiled=True)
    weight_context = collect_band(weight_rows, 0, reach_slabs)
    own_plane_ids = space_index * planes_dev + jnp.arange(planes_dev, dtype=jnp.int32)
    plane_taper = taper_of(own_plane_ids, context_planes, planes_all, reach_planes)

    def plane_gain(taper_row):
        return jnp.dot(context_anom * taper_row[None, :], weight_context, precision=highest)

    gain_blocks = lax.map(plane_gain, plane_taper)
    state_mean = jnp.sum(owned_cells, axis=0) / members
    state_anom = owned_cells - state_mean
    update = jnp.einsum("jxp,xjk->kxp", state_anom, gain_blocks, precision=highest) / (members - 1)
    analysis = owned_cells + update
    return lax.all_to_all(analysis, "mem", split_axis=0, concat_axis=2, tiled=True)


def halves(x):
    high = x.astype(jnp.bfloat16)
    low = (x - high.astype(jnp.float32)).astype(jnp.bfloat16)
    return high, low


def mxu(a, b):
    return jnp.dot(a, b, preferred_element_type=jnp.float32)


def round_up(value, unit):
    return -(-value // unit) * unit


def pack_kernel(ens_ref, forcing_ref, give_ref, keep_ref):
    members_dev, planes_dev, _ = ens_ref.shape
    blocks, rows, width = give_ref.shape
    state_rows = planes_dev * members_dev
    me = lax.axis_index("space")
    tail = jnp.zeros((rows - state_rows - planes_dev, width), jnp.float32)
    for hop in range(blocks):
        for ref, flip in ((give_ref, 1), (keep_ref, 0)):
            first = jnp.bitwise_xor(me, 2 * hop + flip) * width
            span = pl.ds(pl.multiple_of(first, width), width)
            for plane in range(planes_dev):
                top = plane * members_dev
                ref[hop, top : top + members_dev, :] = ens_ref[:, plane, span]
            ref[hop, state_rows:, :] = jnp.concatenate([forcing_ref[:, span], tail], axis=0)


def join_kernel(keep_ref, got_ref, *outs):
    skip = keep_ref.shape[0] - len(outs)
    for hop, out in enumerate(outs):
        out[0] = keep_ref[hop + skip]
        out[1] = got_ref[hop + skip]


def forecast_kernel(*refs, planes_dev, members_dev, slabs):
    keep_ref, got_ref, others = refs[0], refs[1], refs[2 : 1 + slabs // 2]
    own_ref, cross_ref, grid_ref = refs[1 + slabs // 2 :]
    width = own_ref.shape[2]
    state_rows = planes_dev * members_dev
    count = slabs * planes_dev
    me = lax.axis_index("space")
    grid_ref[me] = keep_ref[0]
    grid_ref[jnp.bitwise_xor(me, 1)] = got_ref[0]
    for hop, other in enumerate(others):
        for flip in range(2):
            grid_ref[jnp.bitwise_xor(me, 2 * hop + 2 + flip)] = other[flip]
    for lane in range(0, width, LANES):
        lanes = slice(lane, lane + LANES)
        drive = []
        for plane in range(count):
            row = state_rows + plane % planes_dev
            drive.append(grid_ref[plane // planes_dev, row : row + 1, lanes])
        for member in range(0, members_dev, SUBLANES):
            column = []
            for plane in range(count):
                top = (plane % planes_dev) * members_dev + member
                column.append(grid_ref[plane // planes_dev, top : top + SUBLANES, lanes])
            for _ in range(FSTEPS):
                column = [
                    column[n]
                    + time_step
                    * (
                        (column[(n + 1) % count] - column[n - 2]) * column[n - 1]
                        - column[n]
                        + drive[n]
                    )
                    for n in range(count)
                ]
            for plane in range(count):
                top = (plane % planes_dev) * members_dev + member
                grid_ref[plane // planes_dev, top : top + SUBLANES, lanes] = column[plane]
    for hop in range(slabs // 2):
        own_ref[hop] = grid_ref[jnp.bitwise_xor(me, 2 * hop), :state_rows]
        cross_ref[hop] = grid_ref[jnp.bitwise_xor(me, 2 * hop + 1), :state_rows]


def observe_kernel(*refs, planes_dev, members_dev, plane_cells):
    pieces, (local_ref, out_ref, rest_ref, whole_ref) = refs[:-4], refs[-4:]
    width = rest_ref.shape[2]
    obs_dev = local_ref.shape[1]
    me = lax.axis_index("space")
    local = local_ref[...] - me * (planes_dev * plane_cells)
    total = jnp.zeros((3 * members_dev, obs_dev), jnp.float32)
    for hop, piece in enumerate(pieces):
        for flip in range(2):
            block = jnp.bitwise_xor(me, 2 * hop + flip)
            if hop:
                rest_ref[2 * hop - 2 + flip] = piece[flip]
            whole_ref[2 * hop + flip] = piece[flip]
            for plane in range(planes_dev):
                base = plane * plane_cells + block * width
                index = lax.broadcasted_iota(jnp.int32, (width, obs_dev), 0)
                pick = (index == local - base).astype(jnp.float32).astype(jnp.bfloat16)
                top = plane * members_dev
                values = piece[flip, top : top + members_dev, :]
                high = values.astype(jnp.bfloat16)
                middle, low = halves(values - high.astype(jnp.float32))
                total += mxu(jnp.concatenate([high, middle, low], axis=0), pick)
    out_ref[...] = (
        total[:members_dev]
        + total[members_dev : 2 * members_dev]
        + total[2 * members_dev :]
    )


def stack_kernel(*refs, planes_dev, plane_cells):
    seen, (cell_ref, value_ref, var_ref, noise_ref, out_ref) = refs[:-5], refs[-5:]
    row = 0
    for ref in seen:
        out_ref[row : row + ref.shape[0]] = ref[...]
        row += ref.shape[0]
    wanted = value_ref[...] + jnp.sqrt(var_ref[...]) * noise_ref[...]
    out_ref[row : row + wanted.shape[0]] = wanted
    base = lax.axis_index("space") * planes_dev
    local = cell_ref[...] - base * plane_cells
    place = jnp.zeros(local.shape, jnp.float32) + base.astype(jnp.float32)
    for plane in range(1, planes_dev):
        place = place + jnp.where(local >= plane * plane_cells, 1.0, 0.0)
    fill = jnp.zeros((SUBLANES - 2, local.shape[1]), jnp.float32)
    out_ref[row + wanted.shape[0] :] = jnp.concatenate([var_ref[...], place, fill], axis=0)


def merge_kernel(home_ref, rest_ref, out_ref):
    split = home_ref.shape[0]
    out_ref[:split] = home_ref[...]
    out_ref[split:] = rest_ref[...]


def solve_kernel(*refs, members, members_dev, planes_dev, pair, reach_slabs):
    slabs = len(refs) - 10
    ins, gain_ref = refs[:slabs], refs[slabs]
    anom_ref, flip_ref, side_ref, cov_hi, cov_lo, dir_ref, res_ref, sol_ref, split_ref = refs[
        slabs + 1 :
    ]
    obs_dev = ins[0].shape[1]
    planes_all = planes_dev * slabs
    reach_planes = planes_dev * reach_slabs
    me = lax.axis_index("space")
    member_count = jnp.float32(members)

    for offset in range(slabs):
        slab = jnp.bitwise_xor(me, offset)
        block = ins[offset][...]
        observed = block[:members]
        mean = jnp.sum(observed, axis=0, keepdims=True) / member_count
        anom = observed - mean
        high, low = halves(anom)
        anom_ref[slab, :members] = high
        anom_ref[slab, members : 2 * members] = high
        anom_ref[slab, 2 * members :] = low
        turned = anom.T
        turned_hi, turned_lo = halves(turned)
        flip_ref[slab, :, :members] = turned_hi
        flip_ref[slab, :, members:] = turned_lo
        res_ref[slab] = block[members : members + members_dev] - observed[:members_dev]
        side_ref[slab] = block[members + members_dev : members + members_dev + SUBLANES]

    lower = None
    variances, places, columns = [], [], []
    for slab in range(slabs):
        side = side_ref[slab]
        variances.append(side[0:1])
        places.append(side[1:2])
        columns.append(side.T[:, 1:2])
    var_row = jnp.concatenate(variances, axis=1)
    place_row = jnp.concatenate(places, axis=1)
    lower = jnp.min(var_row, axis=1, keepdims=True)

    tile = pair * obs_dev
    tiles = slabs // pair
    reach_tiles = -(-reach_slabs // pair)
    near = {}
    for right in range(tiles):
        near[right] = sorted({(right + step) % tiles for step in range(-reach_tiles, reach_tiles + 1)})
    scale = jnp.float32(1.0 / (members - 1))
    upper = None
    for right in range(tiles):
        span = slice(right * tile, (right + 1) * tile)
        tops = jnp.concatenate(
            [anom_ref[right * pair + n, : 2 * members] for n in range(pair)], axis=1
        )
        lows = jnp.concatenate(
            [anom_ref[right * pair + n, 2 * members :] for n in range(pair)], axis=1
        )
        along = place_row[:, span]
        sums = None
        for order, left in enumerate(near[right]):
            for part in range(pair):
                slab = left * pair + part
                rows = flip_ref[slab]
                gram = mxu(rows, tops) + mxu(rows[:, :members], lows)
                spread = jnp.abs(columns[slab] - along)
                spread = jnp.minimum(spread, planes_all - spread)
                taper = jnp.maximum(0.0, 1.0 - spread / reach_planes)
                cov = taper * (gram * scale)
                if left == right:
                    below = lax.broadcasted_iota(jnp.int32, (obs_dev, tile), 0) + part * obs_dev
                    across = lax.broadcasted_iota(jnp.int32, (obs_dev, tile), 1)
                    cov = cov + jnp.where(below == across, var_row[:, span], 0.0)
                size = jnp.sum(jnp.abs(cov), axis=0, keepdims=True)
                sums = size if sums is None else sums + size
                high, low = halves(cov)
                top = (order * pair + part) * obs_dev
                cov_hi[right, top : top + obs_dev, :] = high
                cov_lo[right, top : top + obs_dev, :] = low
        biggest = jnp.max(sums, axis=1, keepdims=True)
        upper = biggest if upper is None else jnp.maximum(upper, biggest)

    center = (upper + lower) / 2.0
    radius = (upper - lower) / 2.0
    sigma_ratio = center / radius
    rho_now = 1.0 / sigma_ratio
    for slab in range(slabs):
        span = slice(slab * obs_dev, (slab + 1) * obs_dev)
        start = res_ref[slab] / center
        dir_ref[slab] = start
        sol_ref[slab] = start
        high, low = halves(start)
        split_ref[:members_dev, span] = high
        split_ref[members_dev:, span] = low
    for iteration in range(ITERS - 1):
        rho_next = 1.0 / (2.0 * sigma_ratio - rho_now)
        keep = rho_next * rho_now
        take = 2.0 * rho_next / radius
        images = []
        for right in range(tiles):
            lefts = jnp.concatenate(
                [split_ref[:, left * tile : (left + 1) * tile] for left in near[right]], axis=1
            )
            both = mxu(lefts, cov_hi[right])
            images.append(
                both[:members_dev]
                + both[members_dev:]
                + mxu(lefts[:members_dev], cov_lo[right])
            )
        for slab in range(slabs):
            span = slice(slab * obs_dev, (slab + 1) * obs_dev)
            part = slab % pair
            image = images[slab // pair][:, part * obs_dev : (part + 1) * obs_dev]
            residual = res_ref[slab] - image
            res_ref[slab] = residual
            ahead = keep * dir_ref[slab] + take * residual
            dir_ref[slab] = ahead
            sol_ref[slab] += ahead
            if iteration < ITERS - 2:
                high, low = halves(ahead)
                split_ref[:members_dev, span] = high
                split_ref[members_dev:, span] = low
        rho_now = rho_next

    total = jnp.zeros((2 * planes_dev * members_dev, members), jnp.float32)
    extra = jnp.zeros((planes_dev * members_dev, members), jnp.float32)
    for slab in range(slabs):
        weight = sol_ref[slab]
        tapered = []
        for plane in range(planes_dev):
            own = (me * planes_dev + plane).astype(jnp.float32)
            spread = jnp.abs(own - place_row[:, slab * obs_dev : (slab + 1) * obs_dev])
            spread = jnp.minimum(spread, planes_all - spread)
            tapered.append(weight * jnp.maximum(0.0, 1.0 - spread / reach_planes))
        high, low = halves(jnp.concatenate(tapered, axis=0))
        rows = flip_ref[slab]
        total += mxu(jnp.concatenate([high, low], axis=0), rows[:, :members])
        extra += mxu(high, rows[:, members:])
    half = planes_dev * members_dev
    gain = (total[:half] + total[half:] + extra) * scale
    for plane in range(planes_dev):
        gain_ref[plane] = gain[plane * members_dev : (plane + 1) * members_dev]


def update_kernel(own_ref, home_ref, rest_ref, far_ref, middle_ref, end_ref, gain_ref, out_ref):
    blocks, _, width = own_ref.shape
    members_dev, planes_dev = out_ref.shape[:2]
    split = home_ref.shape[0]
    member_count = jnp.float32(gain_ref.shape[2])
    me = lax.axis_index("space")
    for plane in range(planes_dev):
        high, low = halves(gain_ref[plane])
        both = jnp.concatenate([high, low], axis=0)
        span = slice(plane * members_dev, (plane + 1) * members_dev)
        for block in range(blocks):
            own = own_ref[block, span, :]
            one = home_ref[block, span, :] if block < split else rest_ref[block - split, span, :]
            last = middle_ref[block, span, :] + end_ref[block, span, :]
            values = jnp.concatenate([own, one, far_ref[block, span, :], last], axis=0)
            anom = values - jnp.sum(values, axis=0, keepdims=True) / member_count
            anom_hi, anom_lo = halves(anom)
            change = mxu(both, anom_hi)
            change = change[:members_dev] + change[members_dev:] + mxu(high, anom_lo)
            start = jnp.bitwise_xor(me, block) * width
            out_ref[:, plane, pl.ds(pl.multiple_of(start, width), width)] = own + change


def on_core(kernel, shapes, flops, moved, scratch=(), room=8, in_specs=None):
    single = not isinstance(shapes, list)
    many = [shapes] if single else shapes
    out = [x if hasattr(x, "dtype") else jax.ShapeDtypeStruct(x, jnp.float32) for x in many]
    extra = {} if in_specs is None else {"in_specs": in_specs}
    return pl.pallas_call(
        kernel,
        compiler_params=pltpu.CompilerParams(vmem_limit_bytes=room * 2**20),
        out_shape=out[0] if single else out,
        scratch_shapes=list(scratch),
        cost_estimate=pl.CostEstimate(flops=flops, bytes_accessed=moved, transcendentals=0),
        **extra,
    )


def replicated(ensemble, forcing, obs_cell, obs_value, obs_var, obs_noise):
    members_dev, planes_dev, plane_cells = ensemble.shape
    obs_dev = obs_cell.shape[0]
    slabs = lax.axis_size("space")
    mem_count = lax.axis_size("mem")
    members = members_dev * mem_count
    reach_slabs = min(8, slabs // 4)
    width = plane_cells // slabs
    state_rows = planes_dev * members_dev
    sent_rows = round_up(state_rows + planes_dev, SUBLANES)
    state_bytes = 4 * ensemble.size
    hops = slabs // 2
    sizes = dict(planes_dev=planes_dev, members_dev=members_dev)

    give, keep = on_core(
        pack_kernel, [(hops, sent_rows, width)] * 2, ensemble.size, 2 * state_bytes
    )(ensemble, forcing)
    got = flipped(give, "space", 1)
    sent = on_core(join_kernel, [(2, sent_rows, width)] * (hops - 1), 1, 2 * state_bytes)(keep, got)
    come = [flipped(sent[n - 1], "space", 2 * n) for n in range(1, hops)]
    own, cross = on_core(
        functools.partial(forecast_kernel, slabs=slabs, **sizes),
        [(hops, state_rows, width)] * 2,
        24 * ensemble.size,
        2 * state_bytes,
        scratch=[pltpu.VMEM((slabs, sent_rows, width), jnp.float32)],
    )(keep, got, *come)

    crossed = flipped(cross, "space", 1)
    back = on_core(join_kernel, [(2, state_rows, width)] * hops, 1, 2 * state_bytes)(own, crossed)
    home = back[0]
    pieces = [home] + [flipped(back[n], "space", 2 * n) for n in range(1, hops)]
    home_one = flipped(home, "mem", 1)
    home_two = flipped(home, "mem", 2)
    observed, rest, whole = on_core(
        functools.partial(observe_kernel, plane_cells=plane_cells, **sizes),
        [
            (members_dev, obs_dev),
            (slabs - 2, state_rows, width),
            (slabs, state_rows, width),
        ],
        6 * ensemble.size * obs_dev,
        state_bytes,
    )(*pieces, obs_cell[None])

    seen = [observed] + [flipped(observed, "mem", n) for n in range(1, mem_count)]
    rest_one = flipped(rest, "mem", 1)
    rest_two = flipped(rest, "mem", 2)
    block = on_core(
        functools.partial(stack_kernel, planes_dev=planes_dev, plane_cells=plane_cells),
        (members + members_dev + SUBLANES, obs_dev),
        1,
        8 * members * obs_dev,
    )(*seen, obs_cell[None], obs_value[None], obs_var[None], obs_noise)
    near = [block] + [flipped(block, "space", 2 * n) for n in range(1, hops)]
    gathered = []
    for n in range(hops):
        gathered += [near[n], flipped(near[n], "space", 1)]

    all_middle = lax.ppermute(whole, "mem", [(1, 2), (2, 1)])
    far = on_core(merge_kernel, (slabs, state_rows, width), 1, 2 * state_bytes)(home_two, rest_two)
    all_out = lax.ppermute(far, "mem", [(2, 3), (1, 0)])

    pair = 2
    tiles = slabs // pair
    near_tiles = min(tiles, 1 + 2 * (-(-reach_slabs // pair)))
    tile = pair * obs_dev
    count = slabs * obs_dev
    low_type = jnp.bfloat16
    gain = on_core(
        functools.partial(
            solve_kernel, members=members, pair=pair, reach_slabs=reach_slabs, **sizes
        ),
        (planes_dev, members_dev, members),
        6 * count * count * (members + 2 * ITERS * members_dev),
        4 * count * (members + members_dev),
        [
            pltpu.VMEM((slabs, 3 * members, obs_dev), low_type),
            pltpu.VMEM((slabs, obs_dev, 2 * members), low_type),
            pltpu.VMEM((slabs, SUBLANES, obs_dev), jnp.float32),
            pltpu.VMEM((tiles, near_tiles * tile, tile), low_type),
            pltpu.VMEM((tiles, near_tiles * tile, tile), low_type),
            pltpu.VMEM((slabs, members_dev, obs_dev), jnp.float32),
            pltpu.VMEM((slabs, members_dev, obs_dev), jnp.float32),
            pltpu.VMEM((slabs, members_dev, obs_dev), jnp.float32),
            pltpu.VMEM((2 * members_dev, count), low_type),
        ],
        room=20,
    )(*gathered)

    return on_core(
        update_kernel, ensemble.shape, 6 * ensemble.size * members, 6 * state_bytes, room=12
    )(whole, home_one, rest_one, far, all_middle, all_out, gain)


def shards(ensemble, forcing, obs_cell, obs_value, obs_var, obs_noise):
    args = (ensemble, forcing, obs_cell, obs_value, obs_var, obs_noise)
    members_dev, _, plane_cells = ensemble.shape
    slabs, groups, obs_dev = (lax.axis_size("space"), lax.axis_size("mem"), obs_cell.shape[0])
    aligned = (
        obs_dev % LANES == 0
        and plane_cells % (slabs * LANES) == 0
        and members_dev % SUBLANES == 0
        and (members_dev * groups) % LANES == 0
    )
    small = 4 * (slabs * obs_dev) ** 2 <= 2**24
    paired = slabs & (slabs - 1) == 0 and slabs >= 4
    if aligned and small and paired and groups == 4:
        return replicated(*args)
    return banded(*args)


def solution(mesh):
    placed = (
        P("mem", "space", None),
        P("space", None),
        P("space"),
        P("space"),
        P("space"),
        P("mem", "space"),
    )
    return jax.shard_map(
        shards, mesh=mesh, in_specs=placed, out_specs=P("mem", "space", None), check_vma=False
    )
```

```python
import functools

import jax
import jax.numpy as jnp
from jax import lax
from jax.experimental import pallas as pl
from jax.experimental.pallas import tpu as pltpu
from jax.sharding import PartitionSpec as P


FSTEPS = 4
ITERS = 6
LANES = 128
SUBLANES = 8

time_step = 0.05
highest = lax.Precision.HIGHEST


def from_behind(value, axis, steps):
    count = lax.axis_size(axis)
    pairs = [(source, (source + steps) % count) for source in range(count)]
    return lax.ppermute(value, axis, pairs)


def flipped(value, axis, mask):
    count = lax.axis_size(axis)
    return lax.ppermute(value, axis, [(i, i ^ mask) for i in range(count)])


def padded_2(x, sides, width):
    for axis, dim in sides:
        size, length = (lax.axis_size(axis), x.shape[dim])
        up = [(i, (i + 1) % size) for i in range(size)]
        down = [(j, i) for i, j in up]
        last = lax.slice_in_dim(x, length - width, length, axis=dim)
        initial = lax.slice_in_dim(x, 0, width, axis=dim)
        before = lax.ppermute(last, axis, up)
        after = lax.ppermute(initial, axis, down)
        x = jnp.concatenate([before, x, after], axis=dim)
    return x


def taper_of(planes_a, planes_b, planes_all, reach_planes):
    spread = jnp.abs(planes_a[:, None] - planes_b[None, :])
    spread = jnp.minimum(spread, planes_all - spread)
    return jnp.maximum(0.0, 1.0 - spread.astype(jnp.float32) / reach_planes)


def collect_band(values, along, reach_slabs):
    pieces = []
    for offset in range(-reach_slabs, reach_slabs + 1):
        if offset == 0:
            pieces.append(values)
        else:
            pieces.append(from_behind(values, "space", -offset))
    return jnp.concatenate(pieces, axis=along)


def banded(ensemble, forcing, obs_cell, obs_value, obs_var, obs_noise):
    members_dev, planes_dev, plane_cells = ensemble.shape
    obs_dev = obs_cell.shape[0]
    space_count = lax.axis_size("space")
    mem_count = lax.axis_size("mem")
    space_index = lax.axis_index("space")
    mem_index = lax.axis_index("mem")
    members = members_dev * mem_count
    planes_all = planes_dev * space_count
    reach_slabs = min(8, space_count // 4)
    reach_planes = planes_dev * reach_slabs
    band_width = reach_slabs * obs_dev
    states = ensemble
    for _ in range(FSTEPS):
        padded = padded_2(states, (("space", 1),), 2)
        forward_one = padded[:, 3 : 3 + planes_dev]
        back_one = padded[:, 1 : 1 + planes_dev]
        back_two = padded[:, 0:planes_dev]
        states = states + time_step * ((forward_one - back_two) * back_one - states + forcing)
    slab_cells = planes_dev * plane_cells
    local_cells = obs_cell - space_index * slab_cells
    observed = jnp.take(states.reshape(members_dev, slab_cells), local_cells, axis=1)
    own_planes = obs_cell // plane_cells
    own_rows = lax.all_gather(observed, "mem", axis=0, tiled=True)
    own_mean = jnp.sum(own_rows, axis=0) / members
    own_anom = own_rows - own_mean
    stacked = jnp.concatenate([own_anom, own_planes.astype(jnp.float32)[None, :]], axis=0)
    band = collect_band(stacked, 1, reach_slabs)
    context_anom = band[:members]
    context_planes = band[members].astype(jnp.int32)
    context_count = context_anom.shape[1]
    taper_block = taper_of(own_planes, context_planes, planes_all, reach_planes)
    gram_block = jnp.dot(own_anom.T, context_anom, precision=highest) / (members - 1)
    diagonal = jnp.arange(context_count)[None, :] == (band_width + jnp.arange(obs_dev))[:, None]
    covariance = taper_block * gram_block + jnp.where(diagonal, obs_var[:, None], 0.0)
    row_max = jnp.max(jnp.sum(jnp.abs(covariance), axis=1))
    var_min = jnp.min(obs_var)
    both = lax.pmax((row_max, -var_min), "space")
    upper_bound = both[0]
    lower_bound = -both[1]
    mean_rhs = obs_value - own_mean
    member_anom = lax.dynamic_slice_in_dim(own_anom, mem_index * members_dev, members_dev, 0)
    anom_rhs = (jnp.sqrt(obs_var)[None, :] * obs_noise - member_anom).T
    center = (upper_bound + lower_bound) / 2.0
    radius = (upper_bound - lower_bound) / 2.0
    sigma_ratio = center / radius
    rho_now = 1.0 / sigma_ratio
    resid_anom, resid_mean = (anom_rhs, mean_rhs)
    dir_anom, dir_mean = (anom_rhs / center, mean_rhs / center)
    anom_weight = jnp.zeros_like(anom_rhs)
    mean_weight = jnp.zeros_like(mean_rhs)
    for iteration in range(ITERS):
        anom_weight = anom_weight + dir_anom
        mean_weight = mean_weight + dir_mean
        if iteration < ITERS - 1:
            joined = jnp.concatenate([dir_anom, dir_mean[:, None]], axis=1)
            band_dirs = collect_band(joined, 0, reach_slabs)
            image = jnp.dot(covariance, band_dirs, precision=highest)
            image_anom = image[:, :-1]
            image_mean = image[:, -1]
            resid_anom = resid_anom - image_anom
            resid_mean = resid_mean - image_mean
            rho_next = 1.0 / (2.0 * sigma_ratio - rho_now)
            dir_anom = rho_next * rho_now * dir_anom + 2.0 * rho_next / radius * resid_anom
            dir_mean = rho_next * rho_now * dir_mean + 2.0 * rho_next / radius * resid_mean
            rho_now = rho_next
    weight = anom_weight + mean_weight[:, None]
    owned_cells = lax.all_to_all(states, "mem", split_axis=2, concat_axis=0, tiled=True)
    weight_rows = lax.all_gather(weight, "mem", axis=1, tiled=True)
    weight_context = collect_band(weight_rows, 0, reach_slabs)
    own_plane_ids = space_index * planes_dev + jnp.arange(planes_dev, dtype=jnp.int32)
    plane_taper = taper_of(own_plane_ids, context_planes, planes_all, reach_planes)

    def plane_gain(taper_row):
        return jnp.dot(context_anom * taper_row[None, :], weight_context, precision=highest)

    gain_blocks = lax.map(plane_gain, plane_taper)
    state_mean = jnp.sum(owned_cells, axis=0) / members
    state_anom = owned_cells - state_mean
    update = jnp.einsum("jxp,xjk->kxp", state_anom, gain_blocks, precision=highest) / (members - 1)
    analysis = owned_cells + update
    return lax.all_to_all(analysis, "mem", split_axis=0, concat_axis=2, tiled=True)


def halves(x):
    high = x.astype(jnp.bfloat16)
    low = (x - high.astype(jnp.float32)).astype(jnp.bfloat16)
    return high, low


def mxu(a, b):
    return jnp.dot(a, b, preferred_element_type=jnp.float32)


def round_up(value, unit):
    return -(-value // unit) * unit


def pack_kernel(ens_ref, forcing_ref, give_ref, keep_ref):
    members_dev, planes_dev, _ = ens_ref.shape
    blocks, rows, width = give_ref.shape
    state_rows = planes_dev * members_dev
    me = lax.axis_index("space")
    tail = jnp.zeros((rows - state_rows - planes_dev, width), jnp.float32)
    for hop in range(blocks):
        for ref, flip in ((give_ref, 1), (keep_ref, 0)):
            first = jnp.bitwise_xor(me, 2 * hop + flip) * width
            span = pl.ds(pl.multiple_of(first, width), width)
            for plane in range(planes_dev):
                top = plane * members_dev
                ref[hop, top : top + members_dev, :] = ens_ref[:, plane, span]
            ref[hop, state_rows:, :] = jnp.concatenate([forcing_ref[:, span], tail], axis=0)


def join_kernel(keep_ref, got_ref, *outs):
    skip = keep_ref.shape[0] - len(outs)
    for hop, out in enumerate(outs):
        out[0] = keep_ref[hop + skip]
        out[1] = got_ref[hop + skip]


def forecast_kernel(*refs, planes_dev, members_dev, slabs):
    keep_ref, got_ref, others = refs[0], refs[1], refs[2 : 1 + slabs // 2]
    own_ref, cross_ref, grid_ref = refs[1 + slabs // 2 :]
    width = own_ref.shape[2]
    state_rows = planes_dev * members_dev
    count = slabs * planes_dev
    me = lax.axis_index("space")
    grid_ref[me] = keep_ref[0]
    grid_ref[jnp.bitwise_xor(me, 1)] = got_ref[0]
    for hop, other in enumerate(others):
        for flip in range(2):
            grid_ref[jnp.bitwise_xor(me, 2 * hop + 2 + flip)] = other[flip]
    for lane in range(0, width, LANES):
        lanes = slice(lane, lane + LANES)
        drive = []
        for plane in range(count):
            row = state_rows + plane % planes_dev
            drive.append(grid_ref[plane // planes_dev, row : row + 1, lanes])
        for member in range(0, members_dev, SUBLANES):
            column = []
            for plane in range(count):
                top = (plane % planes_dev) * members_dev + member
                column.append(grid_ref[plane // planes_dev, top : top + SUBLANES, lanes])
            for _ in range(FSTEPS):
                column = [
                    column[n]
                    + time_step
                    * (
                        (column[(n + 1) % count] - column[n - 2]) * column[n - 1]
                        - column[n]
                        + drive[n]
                    )
                    for n in range(count)
                ]
            for plane in range(count):
                top = (plane % planes_dev) * members_dev + member
                grid_ref[plane // planes_dev, top : top + SUBLANES, lanes] = column[plane]
    for hop in range(slabs // 2):
        own_ref[hop] = grid_ref[jnp.bitwise_xor(me, 2 * hop), :state_rows]
        cross_ref[hop] = grid_ref[jnp.bitwise_xor(me, 2 * hop + 1), :state_rows]


def observe_kernel(*refs, planes_dev, members_dev, plane_cells):
    pieces, (local_ref, out_ref, rest_ref, whole_ref) = refs[:-4], refs[-4:]
    width = rest_ref.shape[2]
    obs_dev = local_ref.shape[1]
    me = lax.axis_index("space")
    local = local_ref[...] - me * (planes_dev * plane_cells)
    total = jnp.zeros((3 * members_dev, obs_dev), jnp.float32)
    for hop, piece in enumerate(pieces):
        for flip in range(2):
            block = jnp.bitwise_xor(me, 2 * hop + flip)
            if hop:
                rest_ref[2 * hop - 2 + flip] = piece[flip]
            whole_ref[2 * hop + flip] = piece[flip]
            for plane in range(planes_dev):
                base = plane * plane_cells + block * width
                index = lax.broadcasted_iota(jnp.int32, (width, obs_dev), 0)
                pick = (index == local - base).astype(jnp.float32).astype(jnp.bfloat16)
                top = plane * members_dev
                values = piece[flip, top : top + members_dev, :]
                high = values.astype(jnp.bfloat16)
                middle, low = halves(values - high.astype(jnp.float32))
                total += mxu(jnp.concatenate([high, middle, low], axis=0), pick)
    out_ref[...] = (
        total[:members_dev]
        + total[members_dev : 2 * members_dev]
        + total[2 * members_dev :]
    )


def stack_kernel(*refs, planes_dev, plane_cells):
    seen, (cell_ref, value_ref, var_ref, noise_ref, out_ref) = refs[:-5], refs[-5:]
    group = lax.axis_index("mem")
    mid = jnp.logical_and(group > 0, group < lax.axis_size("mem") - 1)
    own, one, two, three = (ref[...] for ref in seen)
    row = 0
    for values in (own, jnp.where(mid, two, one), jnp.where(mid, one, two), three):
        out_ref[row : row + values.shape[0]] = values
        row += values.shape[0]
    wanted = value_ref[...] + jnp.sqrt(var_ref[...]) * noise_ref[...]
    out_ref[row : row + wanted.shape[0]] = wanted
    base = lax.axis_index("space") * planes_dev
    local = cell_ref[...] - base * plane_cells
    place = jnp.zeros(local.shape, jnp.float32) + base.astype(jnp.float32)
    for plane in range(1, planes_dev):
        place = place + jnp.where(local >= plane * plane_cells, 1.0, 0.0)
    fill = jnp.zeros((SUBLANES - 2, local.shape[1]), jnp.float32)
    out_ref[row + wanted.shape[0] :] = jnp.concatenate([var_ref[...], place, fill], axis=0)


def solve_kernel(*refs, members, members_dev, planes_dev, pair, reach_slabs):
    slabs = len(refs) - 10
    ins, gain_ref = refs[:slabs], refs[slabs]
    anom_ref, flip_ref, side_ref, cov_hi, cov_lo, dir_ref, res_ref, sol_ref, split_ref = refs[
        slabs + 1 :
    ]
    obs_dev = ins[0].shape[1]
    planes_all = planes_dev * slabs
    reach_planes = planes_dev * reach_slabs
    me = lax.axis_index("space")
    member_count = jnp.float32(members)

    for offset in range(slabs):
        slab = jnp.bitwise_xor(me, offset)
        block = ins[offset][...]
        observed = block[:members]
        mean = jnp.sum(observed, axis=0, keepdims=True) / member_count
        anom = observed - mean
        high, low = halves(anom)
        anom_ref[slab, :members] = high
        anom_ref[slab, members : 2 * members] = high
        anom_ref[slab, 2 * members :] = low
        turned = anom.T
        turned_hi, turned_lo = halves(turned)
        flip_ref[slab, :, :members] = turned_hi
        flip_ref[slab, :, members:] = turned_lo
        res_ref[slab] = block[members : members + members_dev] - observed[:members_dev]
        side_ref[slab] = block[members + members_dev : members + members_dev + SUBLANES]

    lower = None
    variances, places, columns = [], [], []
    for slab in range(slabs):
        side = side_ref[slab]
        variances.append(side[0:1])
        places.append(side[1:2])
        columns.append(side.T[:, 1:2])
    var_row = jnp.concatenate(variances, axis=1)
    place_row = jnp.concatenate(places, axis=1)
    lower = jnp.min(var_row, axis=1, keepdims=True)

    tile = pair * obs_dev
    tiles = slabs // pair
    reach_tiles = -(-reach_slabs // pair)
    near = {}
    for right in range(tiles):
        near[right] = sorted({(right + step) % tiles for step in range(-reach_tiles, reach_tiles + 1)})
    scale = jnp.float32(1.0 / (members - 1))
    upper = None
    for right in range(tiles):
        span = slice(right * tile, (right + 1) * tile)
        tops = jnp.concatenate(
            [anom_ref[right * pair + n, : 2 * members] for n in range(pair)], axis=1
        )
        lows = jnp.concatenate(
            [anom_ref[right * pair + n, 2 * members :] for n in range(pair)], axis=1
        )
        along = place_row[:, span]
        sums = None
        for order, left in enumerate(near[right]):
            for part in range(pair):
                slab = left * pair + part
                rows = flip_ref[slab]
                gram = mxu(rows, tops) + mxu(rows[:, :members], lows)
                spread = jnp.abs(columns[slab] - along)
                spread = jnp.minimum(spread, planes_all - spread)
                taper = jnp.maximum(0.0, 1.0 - spread / reach_planes)
                cov = taper * (gram * scale)
                if left == right:
                    below = lax.broadcasted_iota(jnp.int32, (obs_dev, tile), 0) + part * obs_dev
                    across = lax.broadcasted_iota(jnp.int32, (obs_dev, tile), 1)
                    cov = cov + jnp.where(below == across, var_row[:, span], 0.0)
                size = jnp.sum(jnp.abs(cov), axis=0, keepdims=True)
                sums = size if sums is None else sums + size
                high, low = halves(cov)
                top = (order * pair + part) * obs_dev
                cov_hi[right, top : top + obs_dev, :] = high
                cov_lo[right, top : top + obs_dev, :] = low
        biggest = jnp.max(sums, axis=1, keepdims=True)
        upper = biggest if upper is None else jnp.maximum(upper, biggest)

    center = (upper + lower) / 2.0
    radius = (upper - lower) / 2.0
    sigma_ratio = center / radius
    rho_now = 1.0 / sigma_ratio
    for slab in range(slabs):
        span = slice(slab * obs_dev, (slab + 1) * obs_dev)
        start = res_ref[slab] / center
        dir_ref[slab] = start
        sol_ref[slab] = start
        high, low = halves(start)
        split_ref[:members_dev, span] = high
        split_ref[members_dev:, span] = low
    for iteration in range(ITERS - 1):
        rho_next = 1.0 / (2.0 * sigma_ratio - rho_now)
        keep = rho_next * rho_now
        take = 2.0 * rho_next / radius
        images = []
        for right in range(tiles):
            lefts = jnp.concatenate(
                [split_ref[:, left * tile : (left + 1) * tile] for left in near[right]], axis=1
            )
            both = mxu(lefts, cov_hi[right])
            images.append(
                both[:members_dev]
                + both[members_dev:]
                + mxu(lefts[:members_dev], cov_lo[right])
            )
        for slab in range(slabs):
            span = slice(slab * obs_dev, (slab + 1) * obs_dev)
            part = slab % pair
            image = images[slab // pair][:, part * obs_dev : (part + 1) * obs_dev]
            residual = res_ref[slab] - image
            res_ref[slab] = residual
            ahead = keep * dir_ref[slab] + take * residual
            dir_ref[slab] = ahead
            sol_ref[slab] += ahead
            if iteration < ITERS - 2:
                high, low = halves(ahead)
                split_ref[:members_dev, span] = high
                split_ref[members_dev:, span] = low
        rho_now = rho_next

    total = jnp.zeros((2 * planes_dev * members_dev, members), jnp.float32)
    extra = jnp.zeros((planes_dev * members_dev, members), jnp.float32)
    for slab in range(slabs):
        weight = sol_ref[slab]
        tapered = []
        for plane in range(planes_dev):
            own = (me * planes_dev + plane).astype(jnp.float32)
            spread = jnp.abs(own - place_row[:, slab * obs_dev : (slab + 1) * obs_dev])
            spread = jnp.minimum(spread, planes_all - spread)
            tapered.append(weight * jnp.maximum(0.0, 1.0 - spread / reach_planes))
        high, low = halves(jnp.concatenate(tapered, axis=0))
        rows = flip_ref[slab]
        total += mxu(jnp.concatenate([high, low], axis=0), rows[:, :members])
        extra += mxu(high, rows[:, members:])
    half = planes_dev * members_dev
    gain = (total[:half] + total[half:] + extra) * scale
    for plane in range(planes_dev):
        gain_ref[plane] = gain[plane * members_dev : (plane + 1) * members_dev]


def centred(gain_ref, plane):
    gain = gain_ref[plane]
    return halves(gain - jnp.mean(gain, axis=1, keepdims=True))


def early_kernel(home_refs, rest_refs, gain_ref, part_ref, level_ref):
    blocks, _, _ = part_ref.shape
    planes_dev, members_dev = gain_ref.shape[:2]
    split = home_refs[0].shape[0]
    here = len(home_refs) * members_dev
    for plane in range(planes_dev):
        high, low = centred(gain_ref, plane)
        high, low = high[:, :here], low[:, :here]
        both = jnp.concatenate([high, low], axis=0)
        span = slice(plane * members_dev, (plane + 1) * members_dev)
        for block in range(blocks):
            refs, part = (home_refs, block) if block < split else (rest_refs, block - split)
            parts = [ref[part, span, :] for ref in refs]
            values = jnp.concatenate(parts, axis=0)
            level = jnp.sum(values, axis=0, keepdims=True) / jnp.float32(here)
            anom_hi, anom_lo = halves(values - level)
            change = mxu(both, anom_hi)
            change = change[:members_dev] + change[members_dev:] + mxu(high, anom_lo)
            part_ref[block, span, :] = parts[0] + change
            level_ref[block, plane : plane + 1, :] = level


def update_kernel(part_ref, level_ref, middle_ref, outer_ref, gain_ref, out_hbm, out_ref, sems):
    blocks, _, width = part_ref.shape
    members_dev, planes_dev = out_hbm.shape[:2]
    me = lax.axis_index("space")
    factors = []
    for plane in range(planes_dev):
        high, low = centred(gain_ref, plane)
        high, low = high[:, -members_dev:], low[:, -members_dev:]
        factors.append((high, jnp.concatenate([high, low], axis=0)))
    copies = []
    for block in range(blocks):
        for plane in range(planes_dev):
            high, both = factors[plane]
            span = slice(plane * members_dev, (plane + 1) * members_dev)
            values = middle_ref[block, span, :] + outer_ref[block, span, :]
            anom_hi, anom_lo = halves(values - level_ref[block, plane : plane + 1, :])
            change = mxu(both, anom_hi)
            change = change[:members_dev] + change[members_dev:] + mxu(high, anom_lo)
            out_ref[block, :, plane, :] = part_ref[block, span, :] + change
        start = jnp.bitwise_xor(me, block) * width
        target = out_hbm.at[:, :, pl.ds(pl.multiple_of(start, width), width)]
        copies.append(pltpu.make_async_copy(out_ref.at[block], target, sems.at[block]))
        copies[-1].start()
    for copy in copies:
        copy.wait()


def merge_kernel(home_ref, rest_ref, out_ref):
    split = home_ref.shape[0]
    out_ref[:split] = home_ref[...]
    out_ref[split:] = rest_ref[...]


def on_core(kernel, shapes, flops, moved, scratch=(), room=8, **extra):
    single = not isinstance(shapes, list)
    many = [shapes] if single else shapes
    out = [x if hasattr(x, "dtype") else jax.ShapeDtypeStruct(x, jnp.float32) for x in many]
    return pl.pallas_call(
        kernel,
        compiler_params=pltpu.CompilerParams(vmem_limit_bytes=room * 2**20),
        out_shape=out[0] if single else out,
        scratch_shapes=list(scratch),
        cost_estimate=pl.CostEstimate(flops=flops, bytes_accessed=moved, transcendentals=0),
        **extra,
    )


def replicated(ensemble, forcing, obs_cell, obs_value, obs_var, obs_noise):
    members_dev, planes_dev, plane_cells = ensemble.shape
    obs_dev = obs_cell.shape[0]
    slabs = lax.axis_size("space")
    mem_count = lax.axis_size("mem")
    members = members_dev * mem_count
    reach_slabs = min(8, slabs // 4)
    width = plane_cells // slabs
    state_rows = planes_dev * members_dev
    sent_rows = round_up(state_rows + planes_dev, SUBLANES)
    state_bytes = 4 * ensemble.size
    hops = slabs // 2
    sizes = dict(planes_dev=planes_dev, members_dev=members_dev)

    give, keep = on_core(
        pack_kernel, [(hops, sent_rows, width)] * 2, ensemble.size, 2 * state_bytes
    )(ensemble, forcing)
    got = flipped(give, "space", 1)
    sent = on_core(join_kernel, [(2, sent_rows, width)] * (hops - 1), 1, 2 * state_bytes)(keep, got)
    come = [flipped(sent[n - 1], "space", 2 * n) for n in range(1, hops)]
    own, cross = on_core(
        functools.partial(forecast_kernel, slabs=slabs, **sizes),
        [(hops, state_rows, width)] * 2,
        24 * ensemble.size,
        2 * state_bytes,
        scratch=[pltpu.VMEM((slabs, sent_rows, width), jnp.float32)],
    )(keep, got, *come)

    crossed = flipped(cross, "space", 1)
    back = on_core(join_kernel, [(2, state_rows, width)] * hops, 1, 2 * state_bytes)(own, crossed)
    home = back[0]
    pieces = [home] + [flipped(back[n], "space", 2 * n) for n in range(1, hops)]
    leading = [(0, 2), (3, 1), (1, 0), (2, 3)]
    trailing = [(0, 1), (3, 2), (1, 3), (2, 0)]
    outward = [(1, 0), (2, 3)]
    home_lead = lax.ppermute(home, "mem", leading)
    home_trail = lax.ppermute(home, "mem", trailing)
    observed, rest, whole = on_core(
        functools.partial(observe_kernel, plane_cells=plane_cells, **sizes),
        [
            (members_dev, obs_dev),
            (slabs - 2, state_rows, width),
            (slabs, state_rows, width),
        ],
        6 * ensemble.size * obs_dev,
        state_bytes,
    )(*pieces, obs_cell[None])

    seen = [observed] + [flipped(observed, "mem", n) for n in range(1, mem_count)]
    rest_lead = lax.ppermute(rest, "mem", leading)
    rest_trail = lax.ppermute(rest, "mem", trailing)
    block = on_core(
        functools.partial(stack_kernel, planes_dev=planes_dev, plane_cells=plane_cells),
        (members + members_dev + SUBLANES, obs_dev),
        1,
        8 * members * obs_dev,
    )(*seen, obs_cell[None], obs_value[None], obs_var[None], obs_noise)
    near = [block] + [flipped(block, "space", 2 * n) for n in range(1, hops)]
    gathered = []
    for n in range(hops):
        gathered += [near[n], flipped(near[n], "space", 1)]

    all_middle = lax.ppermute(whole, "mem", [(1, 2), (2, 1)])
    passed = on_core(merge_kernel, (slabs, state_rows, width), 1, 2 * state_bytes)(
        home_lead, rest_lead
    )
    all_out = lax.ppermute(passed, "mem", outward)

    pair = 2
    tiles = slabs // pair
    near_tiles = min(tiles, 1 + 2 * (-(-reach_slabs // pair)))
    tile = pair * obs_dev
    count = slabs * obs_dev
    low_type = jnp.bfloat16
    gain = on_core(
        functools.partial(
            solve_kernel, members=members, pair=pair, reach_slabs=reach_slabs, **sizes
        ),
        (planes_dev, members_dev, members),
        6 * count * count * (members + 2 * ITERS * members_dev),
        4 * count * (members + members_dev),
        [
            pltpu.VMEM((slabs, 3 * members, obs_dev), low_type),
            pltpu.VMEM((slabs, obs_dev, 2 * members), low_type),
            pltpu.VMEM((slabs, SUBLANES, obs_dev), jnp.float32),
            pltpu.VMEM((tiles, near_tiles * tile, tile), low_type),
            pltpu.VMEM((tiles, near_tiles * tile, tile), low_type),
            pltpu.VMEM((slabs, members_dev, obs_dev), jnp.float32),
            pltpu.VMEM((slabs, members_dev, obs_dev), jnp.float32),
            pltpu.VMEM((slabs, members_dev, obs_dev), jnp.float32),
            pltpu.VMEM((2 * members_dev, count), low_type),
        ],
        room=20,
    )(*gathered)

    part, level = on_core(
        lambda *refs: early_kernel(refs[0:3], refs[3:6], *refs[6:]),
        [(slabs, state_rows, width), (slabs, SUBLANES, width)],
        4 * ensemble.size * members,
        4 * state_bytes,
        room=12,
    )(home, home_lead, home_trail, rest, rest_lead, rest_trail, gain)
    return on_core(
        update_kernel,
        ensemble.shape,
        2 * ensemble.size * members,
        4 * state_bytes,
        [
            pltpu.VMEM((slabs, members_dev, planes_dev, width), jnp.float32),
            pltpu.SemaphoreType.DMA((slabs,)),
        ],
        room=12,
        out_specs=pl.BlockSpec(memory_space=pltpu.HBM),
    )(part, level, all_middle, all_out, gain)


def shards(ensemble, forcing, obs_cell, obs_value, obs_var, obs_noise):
    args = (ensemble, forcing, obs_cell, obs_value, obs_var, obs_noise)
    members_dev, _, plane_cells = ensemble.shape
    slabs, groups, obs_dev = (lax.axis_size("space"), lax.axis_size("mem"), obs_cell.shape[0])
    aligned = (
        obs_dev % LANES == 0
        and plane_cells % (slabs * LANES) == 0
        and members_dev % SUBLANES == 0
        and (members_dev * groups) % LANES == 0
    )
    small = 4 * (slabs * obs_dev) ** 2 <= 2**24
    paired = slabs & (slabs - 1) == 0 and slabs >= 4
    if aligned and small and paired and groups == 4:
        return replicated(*args)
    return banded(*args)


def solution(mesh):
    placed = (
        P("mem", "space", None),
        P("space", None),
        P("space"),
        P("space"),
        P("space"),
        P("mem", "space"),
    )
    return jax.shard_map(
        shards, mesh=mesh, in_specs=placed, out_specs=P("mem", "space", None), check_vma=False
    )
```

```python
import functools

import jax
import jax.numpy as jnp
from jax import lax
from jax.experimental import pallas as pl
from jax.experimental.pallas import tpu as pltpu
from jax.sharding import PartitionSpec as P


FSTEPS = 4
ITERS = 6
LANES = 128
SUBLANES = 8

time_step = 0.05
highest = lax.Precision.HIGHEST


def from_behind(value, axis, steps):
    count = lax.axis_size(axis)
    pairs = [(source, (source + steps) % count) for source in range(count)]
    return lax.ppermute(value, axis, pairs)


def flipped(value, axis, mask):
    count = lax.axis_size(axis)
    return lax.ppermute(value, axis, [(i, i ^ mask) for i in range(count)])


def padded_2(x, sides, width):
    for axis, dim in sides:
        size, length = (lax.axis_size(axis), x.shape[dim])
        up = [(i, (i + 1) % size) for i in range(size)]
        down = [(j, i) for i, j in up]
        last = lax.slice_in_dim(x, length - width, length, axis=dim)
        initial = lax.slice_in_dim(x, 0, width, axis=dim)
        before = lax.ppermute(last, axis, up)
        after = lax.ppermute(initial, axis, down)
        x = jnp.concatenate([before, x, after], axis=dim)
    return x


def taper_of(planes_a, planes_b, planes_all, reach_planes):
    spread = jnp.abs(planes_a[:, None] - planes_b[None, :])
    spread = jnp.minimum(spread, planes_all - spread)
    return jnp.maximum(0.0, 1.0 - spread.astype(jnp.float32) / reach_planes)


def collect_band(values, along, reach_slabs):
    pieces = []
    for offset in range(-reach_slabs, reach_slabs + 1):
        if offset == 0:
            pieces.append(values)
        else:
            pieces.append(from_behind(values, "space", -offset))
    return jnp.concatenate(pieces, axis=along)


def banded(ensemble, forcing, obs_cell, obs_value, obs_var, obs_noise):
    members_dev, planes_dev, plane_cells = ensemble.shape
    obs_dev = obs_cell.shape[0]
    space_count = lax.axis_size("space")
    mem_count = lax.axis_size("mem")
    space_index = lax.axis_index("space")
    mem_index = lax.axis_index("mem")
    members = members_dev * mem_count
    planes_all = planes_dev * space_count
    reach_slabs = min(8, space_count // 4)
    reach_planes = planes_dev * reach_slabs
    band_width = reach_slabs * obs_dev
    states = ensemble
    for _ in range(FSTEPS):
        padded = padded_2(states, (("space", 1),), 2)
        forward_one = padded[:, 3 : 3 + planes_dev]
        back_one = padded[:, 1 : 1 + planes_dev]
        back_two = padded[:, 0:planes_dev]
        states = states + time_step * ((forward_one - back_two) * back_one - states + forcing)
    slab_cells = planes_dev * plane_cells
    local_cells = obs_cell - space_index * slab_cells
    observed = jnp.take(states.reshape(members_dev, slab_cells), local_cells, axis=1)
    own_planes = obs_cell // plane_cells
    own_rows = lax.all_gather(observed, "mem", axis=0, tiled=True)
    own_mean = jnp.sum(own_rows, axis=0) / members
    own_anom = own_rows - own_mean
    stacked = jnp.concatenate([own_anom, own_planes.astype(jnp.float32)[None, :]], axis=0)
    band = collect_band(stacked, 1, reach_slabs)
    context_anom = band[:members]
    context_planes = band[members].astype(jnp.int32)
    context_count = context_anom.shape[1]
    taper_block = taper_of(own_planes, context_planes, planes_all, reach_planes)
    gram_block = jnp.dot(own_anom.T, context_anom, precision=highest) / (members - 1)
    diagonal = jnp.arange(context_count)[None, :] == (band_width + jnp.arange(obs_dev))[:, None]
    covariance = taper_block * gram_block + jnp.where(diagonal, obs_var[:, None], 0.0)
    row_max = jnp.max(jnp.sum(jnp.abs(covariance), axis=1))
    var_min = jnp.min(obs_var)
    both = lax.pmax((row_max, -var_min), "space")
    upper_bound = both[0]
    lower_bound = -both[1]
    mean_rhs = obs_value - own_mean
    member_anom = lax.dynamic_slice_in_dim(own_anom, mem_index * members_dev, members_dev, 0)
    anom_rhs = (jnp.sqrt(obs_var)[None, :] * obs_noise - member_anom).T
    center = (upper_bound + lower_bound) / 2.0
    radius = (upper_bound - lower_bound) / 2.0
    sigma_ratio = center / radius
    rho_now = 1.0 / sigma_ratio
    resid_anom, resid_mean = (anom_rhs, mean_rhs)
    dir_anom, dir_mean = (anom_rhs / center, mean_rhs / center)
    anom_weight = jnp.zeros_like(anom_rhs)
    mean_weight = jnp.zeros_like(mean_rhs)
    for iteration in range(ITERS):
        anom_weight = anom_weight + dir_anom
        mean_weight = mean_weight + dir_mean
        if iteration < ITERS - 1:
            joined = jnp.concatenate([dir_anom, dir_mean[:, None]], axis=1)
            band_dirs = collect_band(joined, 0, reach_slabs)
            image = jnp.dot(covariance, band_dirs, precision=highest)
            image_anom = image[:, :-1]
            image_mean = image[:, -1]
            resid_anom = resid_anom - image_anom
            resid_mean = resid_mean - image_mean
            rho_next = 1.0 / (2.0 * sigma_ratio - rho_now)
            dir_anom = rho_next * rho_now * dir_anom + 2.0 * rho_next / radius * resid_anom
            dir_mean = rho_next * rho_now * dir_mean + 2.0 * rho_next / radius * resid_mean
            rho_now = rho_next
    weight = anom_weight + mean_weight[:, None]
    owned_cells = lax.all_to_all(states, "mem", split_axis=2, concat_axis=0, tiled=True)
    weight_rows = lax.all_gather(weight, "mem", axis=1, tiled=True)
    weight_context = collect_band(weight_rows, 0, reach_slabs)
    own_plane_ids = space_index * planes_dev + jnp.arange(planes_dev, dtype=jnp.int32)
    plane_taper = taper_of(own_plane_ids, context_planes, planes_all, reach_planes)

    def plane_gain(taper_row):
        return jnp.dot(context_anom * taper_row[None, :], weight_context, precision=highest)

    gain_blocks = lax.map(plane_gain, plane_taper)
    state_mean = jnp.sum(owned_cells, axis=0) / members
    state_anom = owned_cells - state_mean
    update = jnp.einsum("jxp,xjk->kxp", state_anom, gain_blocks, precision=highest) / (members - 1)
    analysis = owned_cells + update
    return lax.all_to_all(analysis, "mem", split_axis=0, concat_axis=2, tiled=True)


def halves(x):
    high = x.astype(jnp.bfloat16)
    low = (x - high.astype(jnp.float32)).astype(jnp.bfloat16)
    return high, low


def mxu(a, b):
    return jnp.dot(a, b, preferred_element_type=jnp.float32)


def round_up(value, unit):
    return -(-value // unit) * unit


def pack_kernel(*refs, count):
    sources, refs = refs[:count], refs[count:]
    give_ref, keep_ref, side_ref, local_ref, *targets, sems = refs
    copies = [
        pltpu.make_async_copy(source, target, sems.at[n])
        for n, (source, target) in enumerate(zip(sources, targets))
    ]
    for copy in copies:
        copy.start()
    ens_ref, forcing_ref, cell_ref, value_ref, var_ref, noise_ref = targets
    members_dev, planes_dev, cells = ens_ref.shape
    blocks, rows, width = give_ref.shape
    state_rows = planes_dev * members_dev
    me = lax.axis_index("space")
    for copy in copies:
        copy.wait()
    tail = jnp.zeros((rows - state_rows - planes_dev, width), jnp.float32)
    for hop in range(blocks):
        for ref, flip in ((give_ref, 1), (keep_ref, 0)):
            first = jnp.bitwise_xor(me, 2 * hop + flip) * width
            span = pl.ds(pl.multiple_of(first, width), width)
            for plane in range(planes_dev):
                top = plane * members_dev
                ref[hop, top : top + members_dev, :] = ens_ref[:, plane, span]
            ref[hop, state_rows:, :] = jnp.concatenate([forcing_ref[:, span], tail], axis=0)
    local = cell_ref[...] - me * (planes_dev * cells)
    local_ref[...] = local
    side_ref[:members_dev] = value_ref[...] + jnp.sqrt(var_ref[...]) * noise_ref[...]
    place = jnp.zeros(local.shape, jnp.float32) + (me * planes_dev).astype(jnp.float32)
    for plane in range(1, planes_dev):
        place = place + jnp.where(local >= plane * cells, 1.0, 0.0)
    fill = jnp.zeros((SUBLANES - 2, local.shape[1]), jnp.float32)
    side_ref[members_dev:] = jnp.concatenate([var_ref[...], place, fill], axis=0)


def join_kernel(keep_ref, got_ref, *outs):
    skip = keep_ref.shape[0] - len(outs)
    for hop, out in enumerate(outs):
        out[0] = keep_ref[hop + skip]
        out[1] = got_ref[hop + skip]


def forecast_kernel(*refs, planes_dev, members_dev, slabs):
    keep_ref, got_ref, others = refs[0], refs[1], refs[2 : 1 + slabs // 2]
    own_ref, cross_ref, grid_ref = refs[1 + slabs // 2 :]
    width = own_ref.shape[2]
    state_rows = planes_dev * members_dev
    count = slabs * planes_dev
    me = lax.axis_index("space")
    grid_ref[me] = keep_ref[0]
    grid_ref[jnp.bitwise_xor(me, 1)] = got_ref[0]
    for hop, other in enumerate(others):
        for flip in range(2):
            grid_ref[jnp.bitwise_xor(me, 2 * hop + 2 + flip)] = other[flip]
    for lane in range(0, width, LANES):
        lanes = slice(lane, lane + LANES)
        drive = []
        for plane in range(count):
            row = state_rows + plane % planes_dev
            drive.append(grid_ref[plane // planes_dev, row : row + 1, lanes])
        for member in range(0, members_dev, SUBLANES):
            column = []
            for plane in range(count):
                top = (plane % planes_dev) * members_dev + member
                column.append(grid_ref[plane // planes_dev, top : top + SUBLANES, lanes])
            for _ in range(FSTEPS):
                column = [
                    column[n]
                    + time_step
                    * (
                        (column[(n + 1) % count] - column[n - 2]) * column[n - 1]
                        - column[n]
                        + drive[n]
                    )
                    for n in range(count)
                ]
            for plane in range(count):
                top = (plane % planes_dev) * members_dev + member
                grid_ref[plane // planes_dev, top : top + SUBLANES, lanes] = column[plane]
    for hop in range(slabs // 2):
        own_ref[hop] = grid_ref[jnp.bitwise_xor(me, 2 * hop), :state_rows]
        cross_ref[hop] = grid_ref[jnp.bitwise_xor(me, 2 * hop + 1), :state_rows]


def observe_kernel(*refs, planes_dev, members_dev, plane_cells):
    pieces, (local_ref, out_ref, rest_ref, whole_ref) = refs[:-4], refs[-4:]
    width = rest_ref.shape[2]
    obs_dev = local_ref.shape[1]
    me = lax.axis_index("space")
    local = local_ref[...]
    total = jnp.zeros((3 * members_dev, obs_dev), jnp.float32)
    for hop, piece in enumerate(pieces):
        for flip in range(2):
            block = jnp.bitwise_xor(me, 2 * hop + flip)
            if hop:
                rest_ref[2 * hop - 2 + flip] = piece[flip]
            whole_ref[2 * hop + flip] = piece[flip]
            for plane in range(planes_dev):
                base = plane * plane_cells + block * width
                index = lax.broadcasted_iota(jnp.int32, (width, obs_dev), 0)
                pick = (index == local - base).astype(jnp.float32).astype(jnp.bfloat16)
                top = plane * members_dev
                values = piece[flip, top : top + members_dev, :]
                high = values.astype(jnp.bfloat16)
                middle, low = halves(values - high.astype(jnp.float32))
                total += mxu(jnp.concatenate([high, middle, low], axis=0), pick)
    out_ref[...] = (
        total[:members_dev]
        + total[members_dev : 2 * members_dev]
        + total[2 * members_dev :]
    )


def stack_kernel(own_ref, one_ref, two_ref, three_ref, side_ref, out_ref):
    group = lax.axis_index("mem")
    mid = jnp.logical_and(group > 0, group < lax.axis_size("mem") - 1)
    one, two = one_ref[...], two_ref[...]
    ordered = (own_ref[...], jnp.where(mid, two, one), jnp.where(mid, one, two), three_ref[...])
    row = 0
    for values in (*ordered, side_ref[...]):
        out_ref[row : row + values.shape[0]] = values
        row += values.shape[0]


def solve_kernel(*refs, members, members_dev, planes_dev, pair, reach_slabs):
    slabs = len(refs) - 10
    ins, gain_ref = refs[:slabs], refs[slabs]
    anom_ref, flip_ref, side_ref, cov_hi, cov_lo, dir_ref, res_ref, sol_ref, split_ref = refs[
        slabs + 1 :
    ]
    obs_dev = ins[0].shape[1]
    planes_all = planes_dev * slabs
    reach_planes = planes_dev * reach_slabs
    me = lax.axis_index("space")
    member_count = jnp.float32(members)

    for offset in range(slabs):
        slab = jnp.bitwise_xor(me, offset)
        block = ins[offset][...]
        observed = block[:members]
        mean = jnp.sum(observed, axis=0, keepdims=True) / member_count
        anom = observed - mean
        high, low = halves(anom)
        anom_ref[slab, :members] = high
        anom_ref[slab, members : 2 * members] = high
        anom_ref[slab, 2 * members :] = low
        turned = anom.T
        turned_hi, turned_lo = halves(turned)
        flip_ref[slab, :, :members] = turned_hi
        flip_ref[slab, :, members:] = turned_lo
        res_ref[slab] = block[members : members + members_dev] - observed[:members_dev]
        side_ref[slab] = block[members + members_dev : members + members_dev + SUBLANES]

    lower = None
    variances, places, columns = [], [], []
    for slab in range(slabs):
        side = side_ref[slab]
        variances.append(side[0:1])
        places.append(side[1:2])
        columns.append(side.T[:, 1:2])
    var_row = jnp.concatenate(variances, axis=1)
    place_row = jnp.concatenate(places, axis=1)
    lower = jnp.min(var_row, axis=1, keepdims=True)

    tile = pair * obs_dev
    tiles = slabs // pair
    reach_tiles = -(-reach_slabs // pair)
    near = {}
    for right in range(tiles):
        near[right] = sorted({(right + step) % tiles for step in range(-reach_tiles, reach_tiles + 1)})
    scale = jnp.float32(1.0 / (members - 1))
    upper = None
    for right in range(tiles):
        span = slice(right * tile, (right + 1) * tile)
        tops = jnp.concatenate(
            [anom_ref[right * pair + n, : 2 * members] for n in range(pair)], axis=1
        )
        lows = jnp.concatenate(
            [anom_ref[right * pair + n, 2 * members :] for n in range(pair)], axis=1
        )
        along = place_row[:, span]
        sums = None
        for order, left in enumerate(near[right]):
            for part in range(pair):
                slab = left * pair + part
                rows = flip_ref[slab]
                gram = mxu(rows, tops) + mxu(rows[:, :members], lows)
                spread = jnp.abs(columns[slab] - along)
                spread = jnp.minimum(spread, planes_all - spread)
                taper = jnp.maximum(0.0, 1.0 - spread / reach_planes)
                cov = taper * (gram * scale)
                if left == right:
                    below = lax.broadcasted_iota(jnp.int32, (obs_dev, tile), 0) + part * obs_dev
                    across = lax.broadcasted_iota(jnp.int32, (obs_dev, tile), 1)
                    cov = cov + jnp.where(below == across, var_row[:, span], 0.0)
                size = jnp.sum(jnp.abs(cov), axis=0, keepdims=True)
                sums = size if sums is None else sums + size
                high, low = halves(cov)
                top = (order * pair + part) * obs_dev
                cov_hi[right, top : top + obs_dev, :] = high
                cov_lo[right, top : top + obs_dev, :] = low
        biggest = jnp.max(sums, axis=1, keepdims=True)
        upper = biggest if upper is None else jnp.maximum(upper, biggest)

    center = (upper + lower) / 2.0
    radius = (upper - lower) / 2.0
    sigma_ratio = center / radius
    rho_now = 1.0 / sigma_ratio
    for slab in range(slabs):
        span = slice(slab * obs_dev, (slab + 1) * obs_dev)
        start = res_ref[slab] / center
        dir_ref[slab] = start
        sol_ref[slab] = start
        high, low = halves(start)
        split_ref[:members_dev, span] = high
        split_ref[members_dev:, span] = low
    for iteration in range(ITERS - 1):
        rho_next = 1.0 / (2.0 * sigma_ratio - rho_now)
        keep = rho_next * rho_now
        take = 2.0 * rho_next / radius
        images = []
        for right in range(tiles):
            lefts = jnp.concatenate(
                [split_ref[:, left * tile : (left + 1) * tile] for left in near[right]], axis=1
            )
            both = mxu(lefts, cov_hi[right])
            images.append(
                both[:members_dev]
                + both[members_dev:]
                + mxu(lefts[:members_dev], cov_lo[right])
            )
        for slab in range(slabs):
            span = slice(slab * obs_dev, (slab + 1) * obs_dev)
            part = slab % pair
            image = images[slab // pair][:, part * obs_dev : (part + 1) * obs_dev]
            residual = res_ref[slab] - image
            res_ref[slab] = residual
            ahead = keep * dir_ref[slab] + take * residual
            dir_ref[slab] = ahead
            sol_ref[slab] += ahead
            if iteration < ITERS - 2:
                high, low = halves(ahead)
                split_ref[:members_dev, span] = high
                split_ref[members_dev:, span] = low
        rho_now = rho_next

    total = jnp.zeros((2 * planes_dev * members_dev, members), jnp.float32)
    extra = jnp.zeros((planes_dev * members_dev, members), jnp.float32)
    for slab in range(slabs):
        weight = sol_ref[slab]
        tapered = []
        for plane in range(planes_dev):
            own = (me * planes_dev + plane).astype(jnp.float32)
            spread = jnp.abs(own - place_row[:, slab * obs_dev : (slab + 1) * obs_dev])
            spread = jnp.minimum(spread, planes_all - spread)
            tapered.append(weight * jnp.maximum(0.0, 1.0 - spread / reach_planes))
        high, low = halves(jnp.concatenate(tapered, axis=0))
        rows = flip_ref[slab]
        total += mxu(jnp.concatenate([high, low], axis=0), rows[:, :members])
        extra += mxu(high, rows[:, members:])
    half = planes_dev * members_dev
    gain = (total[:half] + total[half:] + extra) * scale
    for plane in range(planes_dev):
        gain_ref[plane] = gain[plane * members_dev : (plane + 1) * members_dev]


def centred(gain_ref, plane):
    gain = gain_ref[plane]
    return halves(gain - jnp.mean(gain, axis=1, keepdims=True))


def early_kernel(home_refs, rest_refs, gain_ref, part_ref, level_ref):
    blocks, _, _ = part_ref.shape
    planes_dev, members_dev = gain_ref.shape[:2]
    split = home_refs[0].shape[0]
    here = len(home_refs) * members_dev
    for plane in range(planes_dev):
        high, low = centred(gain_ref, plane)
        high, low = high[:, :here], low[:, :here]
        both = jnp.concatenate([high, low], axis=0)
        span = slice(plane * members_dev, (plane + 1) * members_dev)
        for block in range(blocks):
            refs, part = (home_refs, block) if block < split else (rest_refs, block - split)
            parts = [ref[part, span, :] for ref in refs]
            values = jnp.concatenate(parts, axis=0)
            level = jnp.sum(values, axis=0, keepdims=True) / jnp.float32(here)
            anom_hi, anom_lo = halves(values - level)
            change = mxu(both, anom_hi)
            change = change[:members_dev] + change[members_dev:] + mxu(high, anom_lo)
            part_ref[block, span, :] = parts[0] + change
            level_ref[block, plane : plane + 1, :] = level


def update_kernel(part_ref, level_ref, middle_ref, outer_ref, gain_ref, out_hbm, out_ref, sems):
    blocks, _, width = part_ref.shape
    members_dev, planes_dev = out_hbm.shape[:2]
    me = lax.axis_index("space")
    factors = []
    for plane in range(planes_dev):
        high, low = centred(gain_ref, plane)
        high, low = high[:, -members_dev:], low[:, -members_dev:]
        factors.append((high, jnp.concatenate([high, low], axis=0)))
    copies = []
    for block in range(blocks):
        for plane in range(planes_dev):
            high, both = factors[plane]
            span = slice(plane * members_dev, (plane + 1) * members_dev)
            values = middle_ref[block, span, :] + outer_ref[block, span, :]
            anom_hi, anom_lo = halves(values - level_ref[block, plane : plane + 1, :])
            change = mxu(both, anom_hi)
            change = change[:members_dev] + change[members_dev:] + mxu(high, anom_lo)
            out_ref[block, :, plane, :] = part_ref[block, span, :] + change
        start = jnp.bitwise_xor(me, block) * width
        target = out_hbm.at[:, :, pl.ds(pl.multiple_of(start, width), width)]
        copies.append(pltpu.make_async_copy(out_ref.at[block], target, sems.at[block]))
        copies[-1].start()
    for copy in copies:
        copy.wait()


def merge_kernel(home_ref, rest_ref, out_ref):
    split = home_ref.shape[0]
    out_ref[:split] = home_ref[...]
    out_ref[split:] = rest_ref[...]


def on_core(kernel, shapes, flops, moved, scratch=(), room=8, **extra):
    single = not isinstance(shapes, list)
    many = [shapes] if single else shapes
    out = [x if hasattr(x, "dtype") else jax.ShapeDtypeStruct(x, jnp.float32) for x in many]
    return pl.pallas_call(
        kernel,
        compiler_params=pltpu.CompilerParams(vmem_limit_bytes=room * 2**20),
        out_shape=out[0] if single else out,
        scratch_shapes=list(scratch),
        cost_estimate=pl.CostEstimate(flops=flops, bytes_accessed=moved, transcendentals=0),
        **extra,
    )


def replicated(ensemble, forcing, obs_cell, obs_value, obs_var, obs_noise):
    members_dev, planes_dev, plane_cells = ensemble.shape
    obs_dev = obs_cell.shape[0]
    slabs = lax.axis_size("space")
    mem_count = lax.axis_size("mem")
    members = members_dev * mem_count
    reach_slabs = min(8, slabs // 4)
    width = plane_cells // slabs
    state_rows = planes_dev * members_dev
    sent_rows = round_up(state_rows + planes_dev, SUBLANES)
    state_bytes = 4 * ensemble.size
    hops = slabs // 2
    sizes = dict(planes_dev=planes_dev, members_dev=members_dev)

    inputs = (ensemble, forcing, obs_cell[None], obs_value[None], obs_var[None], obs_noise)
    inputs = [pltpu.with_memory_space_constraint(x, pltpu.HBM) for x in inputs]
    give, keep, side, local = on_core(
        functools.partial(pack_kernel, count=len(inputs)),
        [
            (hops, sent_rows, width),
            (hops, sent_rows, width),
            (members_dev + SUBLANES, obs_dev),
            jax.ShapeDtypeStruct((1, obs_dev), jnp.int32),
        ],
        ensemble.size,
        2 * state_bytes,
        [pltpu.VMEM(x.shape, x.dtype) for x in inputs]
        + [pltpu.SemaphoreType.DMA((len(inputs),))],
        in_specs=[pl.BlockSpec(memory_space=pltpu.HBM)] * len(inputs),
    )(*inputs)
    got = flipped(give, "space", 1)
    sent = on_core(join_kernel, [(2, sent_rows, width)] * (hops - 1), 1, 2 * state_bytes)(keep, got)
    come = [flipped(sent[n - 1], "space", 2 * n) for n in range(1, hops)]
    own, cross = on_core(
        functools.partial(forecast_kernel, slabs=slabs, **sizes),
        [(hops, state_rows, width)] * 2,
        24 * ensemble.size,
        2 * state_bytes,
        scratch=[pltpu.VMEM((slabs, sent_rows, width), jnp.float32)],
    )(keep, got, *come)

    crossed = flipped(cross, "space", 1)
    back = on_core(join_kernel, [(2, state_rows, width)] * hops, 1, 2 * state_bytes)(own, crossed)
    home = back[0]
    pieces = [home] + [flipped(back[n], "space", 2 * n) for n in range(1, hops)]
    leading = [(0, 2), (3, 1), (1, 0), (2, 3)]
    trailing = [(0, 1), (3, 2), (1, 3), (2, 0)]
    outward = [(1, 0), (2, 3)]
    home_lead = lax.ppermute(home, "mem", leading)
    home_trail = lax.ppermute(home, "mem", trailing)
    observed, rest, whole = on_core(
        functools.partial(observe_kernel, plane_cells=plane_cells, **sizes),
        [
            (members_dev, obs_dev),
            (slabs - 2, state_rows, width),
            (slabs, state_rows, width),
        ],
        6 * ensemble.size * obs_dev,
        state_bytes,
    )(*pieces, local)

    seen = [observed] + [flipped(observed, "mem", n) for n in range(1, mem_count)]
    rest_lead = lax.ppermute(rest, "mem", leading)
    rest_trail = lax.ppermute(rest, "mem", trailing)
    block = on_core(
        stack_kernel, (members + members_dev + SUBLANES, obs_dev), 1, 8 * members * obs_dev
    )(*seen, side)
    near = [block] + [flipped(block, "space", 2 * n) for n in range(1, hops)]
    gathered = []
    for n in range(hops):
        gathered += [near[n], flipped(near[n], "space", 1)]

    all_middle = lax.ppermute(whole, "mem", [(1, 2), (2, 1)])
    passed = on_core(merge_kernel, (slabs, state_rows, width), 1, 2 * state_bytes)(
        home_lead, rest_lead
    )
    all_out = lax.ppermute(passed, "mem", outward)

    pair = 2
    tiles = slabs // pair
    near_tiles = min(tiles, 1 + 2 * (-(-reach_slabs // pair)))
    tile = pair * obs_dev
    count = slabs * obs_dev
    low_type = jnp.bfloat16
    gain = on_core(
        functools.partial(
            solve_kernel, members=members, pair=pair, reach_slabs=reach_slabs, **sizes
        ),
        (planes_dev, members_dev, members),
        6 * count * count * (members + 2 * ITERS * members_dev),
        4 * count * (members + members_dev),
        [
            pltpu.VMEM((slabs, 3 * members, obs_dev), low_type),
            pltpu.VMEM((slabs, obs_dev, 2 * members), low_type),
            pltpu.VMEM((slabs, SUBLANES, obs_dev), jnp.float32),
            pltpu.VMEM((tiles, near_tiles * tile, tile), low_type),
            pltpu.VMEM((tiles, near_tiles * tile, tile), low_type),
            pltpu.VMEM((slabs, members_dev, obs_dev), jnp.float32),
            pltpu.VMEM((slabs, members_dev, obs_dev), jnp.float32),
            pltpu.VMEM((slabs, members_dev, obs_dev), jnp.float32),
            pltpu.VMEM((2 * members_dev, count), low_type),
        ],
        room=20,
    )(*gathered)

    part, level = on_core(
        lambda *refs: early_kernel(refs[0:3], refs[3:6], *refs[6:]),
        [(slabs, state_rows, width), (slabs, SUBLANES, width)],
        4 * ensemble.size * members,
        4 * state_bytes,
        room=12,
    )(home, home_lead, home_trail, rest, rest_lead, rest_trail, gain)
    return on_core(
        update_kernel,
        ensemble.shape,
        2 * ensemble.size * members,
        4 * state_bytes,
        [
            pltpu.VMEM((slabs, members_dev, planes_dev, width), jnp.float32),
            pltpu.SemaphoreType.DMA((slabs,)),
        ],
        room=12,
        out_specs=pl.BlockSpec(memory_space=pltpu.HBM),
    )(part, level, all_middle, all_out, gain)


def shards(ensemble, forcing, obs_cell, obs_value, obs_var, obs_noise):
    args = (ensemble, forcing, obs_cell, obs_value, obs_var, obs_noise)
    members_dev, _, plane_cells = ensemble.shape
    slabs, groups, obs_dev = (lax.axis_size("space"), lax.axis_size("mem"), obs_cell.shape[0])
    aligned = (
        obs_dev % LANES == 0
        and plane_cells % (slabs * LANES) == 0
        and members_dev % SUBLANES == 0
        and (members_dev * groups) % LANES == 0
    )
    small = 4 * (slabs * obs_dev) ** 2 <= 2**24
    paired = slabs & (slabs - 1) == 0 and slabs >= 4
    if aligned and small and paired and groups == 4:
        return replicated(*args)
    return banded(*args)


def solution(mesh):
    placed = (
        P("mem", "space", None),
        P("space", None),
        P("space"),
        P("space"),
        P("space"),
        P("mem", "space"),
    )
    return jax.shard_map(
        shards, mesh=mesh, in_specs=placed, out_specs=P("mem", "space", None), check_vma=False
    )
```

```python
import functools

import jax
import jax.numpy as jnp
from jax import lax
from jax.experimental import pallas as pl
from jax.experimental.pallas import tpu as pltpu
from jax.sharding import PartitionSpec as P


FSTEPS = 4
ITERS = 6
LANES = 128
SUBLANES = 8

time_step = 0.05
highest = lax.Precision.HIGHEST


def from_behind(value, axis, steps):
    count = lax.axis_size(axis)
    pairs = [(source, (source + steps) % count) for source in range(count)]
    return lax.ppermute(value, axis, pairs)


def flipped(value, axis, mask):
    count = lax.axis_size(axis)
    return lax.ppermute(value, axis, [(i, i ^ mask) for i in range(count)])


def padded_2(x, sides, width):
    for axis, dim in sides:
        size, length = (lax.axis_size(axis), x.shape[dim])
        up = [(i, (i + 1) % size) for i in range(size)]
        down = [(j, i) for i, j in up]
        last = lax.slice_in_dim(x, length - width, length, axis=dim)
        initial = lax.slice_in_dim(x, 0, width, axis=dim)
        before = lax.ppermute(last, axis, up)
        after = lax.ppermute(initial, axis, down)
        x = jnp.concatenate([before, x, after], axis=dim)
    return x


def taper_of(planes_a, planes_b, planes_all, reach_planes):
    spread = jnp.abs(planes_a[:, None] - planes_b[None, :])
    spread = jnp.minimum(spread, planes_all - spread)
    return jnp.maximum(0.0, 1.0 - spread.astype(jnp.float32) / reach_planes)


def collect_band(values, along, reach_slabs):
    pieces = []
    for offset in range(-reach_slabs, reach_slabs + 1):
        if offset == 0:
            pieces.append(values)
        else:
            pieces.append(from_behind(values, "space", -offset))
    return jnp.concatenate(pieces, axis=along)


def banded(ensemble, forcing, obs_cell, obs_value, obs_var, obs_noise):
    members_dev, planes_dev, plane_cells = ensemble.shape
    obs_dev = obs_cell.shape[0]
    space_count = lax.axis_size("space")
    mem_count = lax.axis_size("mem")
    space_index = lax.axis_index("space")
    mem_index = lax.axis_index("mem")
    members = members_dev * mem_count
    planes_all = planes_dev * space_count
    reach_slabs = min(8, space_count // 4)
    reach_planes = planes_dev * reach_slabs
    band_width = reach_slabs * obs_dev
    states = ensemble
    for _ in range(FSTEPS):
        padded = padded_2(states, (("space", 1),), 2)
        forward_one = padded[:, 3 : 3 + planes_dev]
        back_one = padded[:, 1 : 1 + planes_dev]
        back_two = padded[:, 0:planes_dev]
        states = states + time_step * ((forward_one - back_two) * back_one - states + forcing)
    slab_cells = planes_dev * plane_cells
    local_cells = obs_cell - space_index * slab_cells
    observed = jnp.take(states.reshape(members_dev, slab_cells), local_cells, axis=1)
    own_planes = obs_cell // plane_cells
    own_rows = lax.all_gather(observed, "mem", axis=0, tiled=True)
    own_mean = jnp.sum(own_rows, axis=0) / members
    own_anom = own_rows - own_mean
    stacked = jnp.concatenate([own_anom, own_planes.astype(jnp.float32)[None, :]], axis=0)
    band = collect_band(stacked, 1, reach_slabs)
    context_anom = band[:members]
    context_planes = band[members].astype(jnp.int32)
    context_count = context_anom.shape[1]
    taper_block = taper_of(own_planes, context_planes, planes_all, reach_planes)
    gram_block = jnp.dot(own_anom.T, context_anom, precision=highest) / (members - 1)
    diagonal = jnp.arange(context_count)[None, :] == (band_width + jnp.arange(obs_dev))[:, None]
    covariance = taper_block * gram_block + jnp.where(diagonal, obs_var[:, None], 0.0)
    row_max = jnp.max(jnp.sum(jnp.abs(covariance), axis=1))
    var_min = jnp.min(obs_var)
    both = lax.pmax((row_max, -var_min), "space")
    upper_bound = both[0]
    lower_bound = -both[1]
    mean_rhs = obs_value - own_mean
    member_anom = lax.dynamic_slice_in_dim(own_anom, mem_index * members_dev, members_dev, 0)
    anom_rhs = (jnp.sqrt(obs_var)[None, :] * obs_noise - member_anom).T
    center = (upper_bound + lower_bound) / 2.0
    radius = (upper_bound - lower_bound) / 2.0
    sigma_ratio = center / radius
    rho_now = 1.0 / sigma_ratio
    resid_anom, resid_mean = (anom_rhs, mean_rhs)
    dir_anom, dir_mean = (anom_rhs / center, mean_rhs / center)
    anom_weight = jnp.zeros_like(anom_rhs)
    mean_weight = jnp.zeros_like(mean_rhs)
    for iteration in range(ITERS):
        anom_weight = anom_weight + dir_anom
        mean_weight = mean_weight + dir_mean
        if iteration < ITERS - 1:
            joined = jnp.concatenate([dir_anom, dir_mean[:, None]], axis=1)
            band_dirs = collect_band(joined, 0, reach_slabs)
            image = jnp.dot(covariance, band_dirs, precision=highest)
            image_anom = image[:, :-1]
            image_mean = image[:, -1]
            resid_anom = resid_anom - image_anom
            resid_mean = resid_mean - image_mean
            rho_next = 1.0 / (2.0 * sigma_ratio - rho_now)
            dir_anom = rho_next * rho_now * dir_anom + 2.0 * rho_next / radius * resid_anom
            dir_mean = rho_next * rho_now * dir_mean + 2.0 * rho_next / radius * resid_mean
            rho_now = rho_next
    weight = anom_weight + mean_weight[:, None]
    owned_cells = lax.all_to_all(states, "mem", split_axis=2, concat_axis=0, tiled=True)
    weight_rows = lax.all_gather(weight, "mem", axis=1, tiled=True)
    weight_context = collect_band(weight_rows, 0, reach_slabs)
    own_plane_ids = space_index * planes_dev + jnp.arange(planes_dev, dtype=jnp.int32)
    plane_taper = taper_of(own_plane_ids, context_planes, planes_all, reach_planes)

    def plane_gain(taper_row):
        return jnp.dot(context_anom * taper_row[None, :], weight_context, precision=highest)

    gain_blocks = lax.map(plane_gain, plane_taper)
    state_mean = jnp.sum(owned_cells, axis=0) / members
    state_anom = owned_cells - state_mean
    update = jnp.einsum("jxp,xjk->kxp", state_anom, gain_blocks, precision=highest) / (members - 1)
    analysis = owned_cells + update
    return lax.all_to_all(analysis, "mem", split_axis=0, concat_axis=2, tiled=True)


def halves(x):
    high = x.astype(jnp.bfloat16)
    low = (x - high.astype(jnp.float32)).astype(jnp.bfloat16)
    return high, low


def mxu(a, b):
    return jnp.dot(a, b, preferred_element_type=jnp.float32)


def round_up(value, unit):
    return -(-value // unit) * unit


def pack_kernel(*refs, count):
    sources, refs = refs[:count], refs[count:]
    give_ref, keep_ref, side_ref, local_ref, *targets, sems = refs
    copies = [
        pltpu.make_async_copy(source, target, sems.at[n])
        for n, (source, target) in enumerate(zip(sources, targets))
    ]
    for copy in copies:
        copy.start()
    ens_ref, forcing_ref, cell_ref, value_ref, var_ref, noise_ref = targets
    members_dev, planes_dev, cells = ens_ref.shape
    blocks, rows, _ = give_ref.shape
    strips = cells // (2 * blocks * LANES)
    state_rows = strips * planes_dev * members_dev
    me = lax.axis_index("space")
    for copy in copies[1:]:
        copy.wait()
    local = cell_ref[...] - me * (planes_dev * cells)
    local_ref[...] = local
    side_ref[:members_dev] = value_ref[...] + jnp.sqrt(var_ref[...]) * noise_ref[...]
    place = jnp.zeros(local.shape, jnp.float32) + (me * planes_dev).astype(jnp.float32)
    for plane in range(1, planes_dev):
        place = place + jnp.where(local >= plane * cells, 1.0, 0.0)
    fill = jnp.zeros((SUBLANES - 2, local.shape[1]), jnp.float32)
    side_ref[members_dev:] = jnp.concatenate([var_ref[...], place, fill], axis=0)
    copies[0].wait()
    tail = jnp.zeros((rows - state_rows - strips * planes_dev, LANES), jnp.float32)
    for hop in range(blocks):
        for ref, flip in ((give_ref, 1), (keep_ref, 0)):
            first = jnp.bitwise_xor(me, 2 * hop + flip) * (strips * LANES)
            drive = []
            for strip in range(strips):
                lanes = pl.ds(pl.multiple_of(first + strip * LANES, LANES), LANES)
                for plane in range(planes_dev):
                    top = (strip * planes_dev + plane) * members_dev
                    ref[hop, top : top + members_dev, :] = ens_ref[:, plane, lanes]
                drive.append(forcing_ref[:, lanes])
            ref[hop, state_rows:, :] = jnp.concatenate(drive + [tail], axis=0)


def join_sent_kernel(keep_ref, got_ref, *outs, state_rows, drive_rows):
    both = (keep_ref, got_ref)
    for hop, out in enumerate(outs):
        for n, ref in enumerate(both):
            out[n * state_rows : (n + 1) * state_rows, :] = ref[hop + 1, :state_rows]
        drive = [ref[hop + 1, state_rows : state_rows + drive_rows] for ref in both]
        spare = out.shape[0] - 2 * (state_rows + drive_rows)
        if spare:
            drive.append(jnp.zeros((spare, LANES), jnp.float32))
        out[2 * state_rows :, :] = jnp.concatenate(drive, axis=0)


def join_kernel(keep_ref, got_ref, *outs):
    for hop, out in enumerate(outs):
        out[0] = keep_ref[hop]
        out[1] = got_ref[hop]


def forecast_kernel(*refs, planes_dev, members_dev, slabs):
    keep_ref, got_ref, others = refs[0], refs[1], refs[2 : 1 + slabs // 2]
    own_ref, cross_ref, grid_ref = refs[1 + slabs // 2 :]
    strips = own_ref.shape[2] // LANES
    strip_rows = planes_dev * members_dev
    state_rows, drive_rows = strips * strip_rows, strips * planes_dev
    count = slabs * planes_dev
    me = lax.axis_index("space")
    grid_ref[me] = keep_ref[0]
    grid_ref[jnp.bitwise_xor(me, 1)] = got_ref[0]
    for hop, other in enumerate(others):
        for flip in range(2):
            slab = jnp.bitwise_xor(me, 2 * hop + 2 + flip)
            grid_ref[slab, :state_rows] = other[flip * state_rows : (flip + 1) * state_rows]
            first = 2 * state_rows + flip * drive_rows
            grid_ref[slab, state_rows : state_rows + drive_rows] = other[first : first + drive_rows]
    for strip in range(strips):
        drive = []
        for plane in range(count):
            row = state_rows + strip * planes_dev + plane % planes_dev
            drive.append(grid_ref[plane // planes_dev, row : row + 1, :])
        for member in range(0, members_dev, SUBLANES):
            tops = [
                strip * strip_rows + (plane % planes_dev) * members_dev + member
                for plane in range(count)
            ]
            column = [
                grid_ref[plane // planes_dev, tops[plane] : tops[plane] + SUBLANES, :]
                for plane in range(count)
            ]
            for _ in range(FSTEPS):
                column = [
                    column[n]
                    + time_step
                    * (
                        (column[(n + 1) % count] - column[n - 2]) * column[n - 1]
                        - column[n]
                        + drive[n]
                    )
                    for n in range(count)
                ]
            for plane in range(count):
                top = tops[plane]
                grid_ref[plane // planes_dev, top : top + SUBLANES, :] = column[plane]
    for hop in range(slabs // 2):
        for ref, flip in ((own_ref, 0), (cross_ref, 1)):
            slab = jnp.bitwise_xor(me, 2 * hop + flip)
            for strip in range(strips):
                rows = slice(strip * strip_rows, (strip + 1) * strip_rows)
                ref[hop, :, strip * LANES : (strip + 1) * LANES] = grid_ref[slab, rows]


def observe_kernel(*refs, planes_dev, members_dev, plane_cells):
    pieces, (local_ref, out_ref, rest_ref, whole_ref) = refs[:-4], refs[-4:]
    width = rest_ref.shape[2]
    obs_dev = local_ref.shape[1]
    me = lax.axis_index("space")
    local = local_ref[...]
    total = jnp.zeros((3 * members_dev, obs_dev), jnp.float32)
    for hop, piece in enumerate(pieces):
        for flip in range(2):
            block = jnp.bitwise_xor(me, 2 * hop + flip)
            if hop:
                rest_ref[2 * hop - 2 + flip] = piece[flip]
            whole_ref[2 * hop + flip] = piece[flip]
            for plane in range(planes_dev):
                base = plane * plane_cells + block * width
                index = lax.broadcasted_iota(jnp.int32, (width, obs_dev), 0)
                pick = (index == local - base).astype(jnp.float32).astype(jnp.bfloat16)
                top = plane * members_dev
                values = piece[flip, top : top + members_dev, :]
                high = values.astype(jnp.bfloat16)
                middle, low = halves(values - high.astype(jnp.float32))
                total += mxu(jnp.concatenate([high, middle, low], axis=0), pick)
    out_ref[...] = (
        total[:members_dev]
        + total[members_dev : 2 * members_dev]
        + total[2 * members_dev :]
    )


def stack_kernel(own_ref, one_ref, two_ref, three_ref, side_ref, out_ref):
    group = lax.axis_index("mem")
    mid = jnp.logical_and(group > 0, group < lax.axis_size("mem") - 1)
    one, two = one_ref[...], two_ref[...]
    ordered = (own_ref[...], jnp.where(mid, two, one), jnp.where(mid, one, two), three_ref[...])
    row = 0
    for values in (*ordered, side_ref[...]):
        out_ref[row : row + values.shape[0]] = values
        row += values.shape[0]


def solve_kernel(*refs, members, members_dev, planes_dev, pair, reach_slabs):
    slabs = len(refs) - 10
    ins, gain_ref = refs[:slabs], refs[slabs]
    anom_ref, flip_ref, side_ref, cov_hi, cov_lo, dir_ref, res_ref, sol_ref, split_ref = refs[
        slabs + 1 :
    ]
    obs_dev = ins[0].shape[1]
    planes_all = planes_dev * slabs
    reach_planes = planes_dev * reach_slabs
    me = lax.axis_index("space")
    member_count = jnp.float32(members)

    for offset in range(slabs):
        slab = jnp.bitwise_xor(me, offset)
        block = ins[offset][...]
        observed = block[:members]
        mean = jnp.sum(observed, axis=0, keepdims=True) / member_count
        anom = observed - mean
        high, low = halves(anom)
        anom_ref[slab, :members] = high
        anom_ref[slab, members : 2 * members] = high
        anom_ref[slab, 2 * members :] = low
        turned = anom.T
        turned_hi, turned_lo = halves(turned)
        flip_ref[slab, :, :members] = turned_hi
        flip_ref[slab, :, members:] = turned_lo
        res_ref[slab] = block[members : members + members_dev] - observed[:members_dev]
        side_ref[slab] = block[members + members_dev : members + members_dev + SUBLANES]

    lower = None
    variances, places, columns = [], [], []
    for slab in range(slabs):
        side = side_ref[slab]
        variances.append(side[0:1])
        places.append(side[1:2])
        columns.append(side.T[:, 1:2])
    var_row = jnp.concatenate(variances, axis=1)
    place_row = jnp.concatenate(places, axis=1)
    lower = jnp.min(var_row, axis=1, keepdims=True)

    tile = pair * obs_dev
    tiles = slabs // pair
    reach_tiles = -(-reach_slabs // pair)
    near = {}
    for right in range(tiles):
        near[right] = sorted({(right + step) % tiles for step in range(-reach_tiles, reach_tiles + 1)})
    scale = jnp.float32(1.0 / (members - 1))
    upper = None
    for right in range(tiles):
        span = slice(right * tile, (right + 1) * tile)
        tops = jnp.concatenate(
            [anom_ref[right * pair + n, : 2 * members] for n in range(pair)], axis=1
        )
        lows = jnp.concatenate(
            [anom_ref[right * pair + n, 2 * members :] for n in range(pair)], axis=1
        )
        along = place_row[:, span]
        sums = None
        for order, left in enumerate(near[right]):
            for part in range(pair):
                slab = left * pair + part
                rows = flip_ref[slab]
                gram = mxu(rows, tops) + mxu(rows[:, :members], lows)
                spread = jnp.abs(columns[slab] - along)
                spread = jnp.minimum(spread, planes_all - spread)
                taper = jnp.maximum(0.0, 1.0 - spread / reach_planes)
                cov = taper * (gram * scale)
                if left == right:
                    below = lax.broadcasted_iota(jnp.int32, (obs_dev, tile), 0) + part * obs_dev
                    across = lax.broadcasted_iota(jnp.int32, (obs_dev, tile), 1)
                    cov = cov + jnp.where(below == across, var_row[:, span], 0.0)
                size = jnp.sum(jnp.abs(cov), axis=0, keepdims=True)
                sums = size if sums is None else sums + size
                high, low = halves(cov)
                top = (order * pair + part) * obs_dev
                cov_hi[right, top : top + obs_dev, :] = high
                cov_lo[right, top : top + obs_dev, :] = low
        biggest = jnp.max(sums, axis=1, keepdims=True)
        upper = biggest if upper is None else jnp.maximum(upper, biggest)

    center = (upper + lower) / 2.0
    radius = (upper - lower) / 2.0
    sigma_ratio = center / radius
    rho_now = 1.0 / sigma_ratio
    for slab in range(slabs):
        span = slice(slab * obs_dev, (slab + 1) * obs_dev)
        start = res_ref[slab] / center
        dir_ref[slab] = start
        sol_ref[slab] = start
        high, low = halves(start)
        split_ref[:members_dev, span] = high
        split_ref[members_dev:, span] = low
    for iteration in range(ITERS - 1):
        rho_next = 1.0 / (2.0 * sigma_ratio - rho_now)
        keep = rho_next * rho_now
        take = 2.0 * rho_next / radius
        images = []
        for right in range(tiles):
            lefts = jnp.concatenate(
                [split_ref[:, left * tile : (left + 1) * tile] for left in near[right]], axis=1
            )
            both = mxu(lefts, cov_hi[right])
            images.append(
                both[:members_dev]
                + both[members_dev:]
                + mxu(lefts[:members_dev], cov_lo[right])
            )
        for slab in range(slabs):
            span = slice(slab * obs_dev, (slab + 1) * obs_dev)
            part = slab % pair
            image = images[slab // pair][:, part * obs_dev : (part + 1) * obs_dev]
            residual = res_ref[slab] - image
            res_ref[slab] = residual
            ahead = keep * dir_ref[slab] + take * residual
            dir_ref[slab] = ahead
            sol_ref[slab] += ahead
            if iteration < ITERS - 2:
                high, low = halves(ahead)
                split_ref[:members_dev, span] = high
                split_ref[members_dev:, span] = low
        rho_now = rho_next

    total = jnp.zeros((2 * planes_dev * members_dev, members), jnp.float32)
    extra = jnp.zeros((planes_dev * members_dev, members), jnp.float32)
    for slab in range(slabs):
        weight = sol_ref[slab]
        tapered = []
        for plane in range(planes_dev):
            own = (me * planes_dev + plane).astype(jnp.float32)
            spread = jnp.abs(own - place_row[:, slab * obs_dev : (slab + 1) * obs_dev])
            spread = jnp.minimum(spread, planes_all - spread)
            tapered.append(weight * jnp.maximum(0.0, 1.0 - spread / reach_planes))
        high, low = halves(jnp.concatenate(tapered, axis=0))
        rows = flip_ref[slab]
        total += mxu(jnp.concatenate([high, low], axis=0), rows[:, :members])
        extra += mxu(high, rows[:, members:])
    half = planes_dev * members_dev
    gain = (total[:half] + total[half:] + extra) * scale
    for plane in range(planes_dev):
        gain_ref[plane] = gain[plane * members_dev : (plane + 1) * members_dev]


def centred(gain_ref, plane):
    gain = gain_ref[plane]
    return halves(gain - jnp.mean(gain, axis=1, keepdims=True))


def early_kernel(home_refs, rest_refs, gain_ref, part_ref, level_ref):
    blocks, _, _ = part_ref.shape
    planes_dev, members_dev = gain_ref.shape[:2]
    split = home_refs[0].shape[0]
    here = len(home_refs) * members_dev
    for plane in range(planes_dev):
        high, low = centred(gain_ref, plane)
        high, low = high[:, :here], low[:, :here]
        both = jnp.concatenate([high, low], axis=0)
        span = slice(plane * members_dev, (plane + 1) * members_dev)
        for block in range(blocks):
            refs, part = (home_refs, block) if block < split else (rest_refs, block - split)
            parts = [ref[part, span, :] for ref in refs]
            values = jnp.concatenate(parts, axis=0)
            level = jnp.sum(values, axis=0, keepdims=True) / jnp.float32(here)
            anom_hi, anom_lo = halves(values - level)
            change = mxu(both, anom_hi)
            change = change[:members_dev] + change[members_dev:] + mxu(high, anom_lo)
            part_ref[block, span, :] = parts[0] + change
            level_ref[block, plane : plane + 1, :] = level


def update_kernel(part_ref, level_ref, middle_ref, outer_ref, gain_ref, out_hbm, out_ref, sems):
    blocks, _, width = part_ref.shape
    members_dev, planes_dev = out_hbm.shape[:2]
    me = lax.axis_index("space")
    factors = []
    for plane in range(planes_dev):
        high, low = centred(gain_ref, plane)
        high, low = high[:, -members_dev:], low[:, -members_dev:]
        factors.append((high, jnp.concatenate([high, low], axis=0)))
    copies = []
    for block in range(blocks):
        for plane in range(planes_dev):
            high, both = factors[plane]
            span = slice(plane * members_dev, (plane + 1) * members_dev)
            values = middle_ref[block, span, :] + outer_ref[block, span, :]
            anom_hi, anom_lo = halves(values - level_ref[block, plane : plane + 1, :])
            change = mxu(both, anom_hi)
            change = change[:members_dev] + change[members_dev:] + mxu(high, anom_lo)
            out_ref[block, :, plane, :] = part_ref[block, span, :] + change
        start = jnp.bitwise_xor(me, block) * width
        target = out_hbm.at[:, :, pl.ds(pl.multiple_of(start, width), width)]
        copies.append(pltpu.make_async_copy(out_ref.at[block], target, sems.at[block]))
        copies[-1].start()
    for copy in copies:
        copy.wait()


def merge_kernel(home_ref, rest_ref, out_ref):
    split = home_ref.shape[0]
    out_ref[:split] = home_ref[...]
    out_ref[split:] = rest_ref[...]


def on_core(kernel, shapes, flops, moved, scratch=(), room=8, **extra):
    single = not isinstance(shapes, list)
    many = [shapes] if single else shapes
    out = [x if hasattr(x, "dtype") else jax.ShapeDtypeStruct(x, jnp.float32) for x in many]
    return pl.pallas_call(
        kernel,
        compiler_params=pltpu.CompilerParams(vmem_limit_bytes=room * 2**20),
        out_shape=out[0] if single else out,
        scratch_shapes=list(scratch),
        cost_estimate=pl.CostEstimate(flops=flops, bytes_accessed=moved, transcendentals=0),
        **extra,
    )


def replicated(ensemble, forcing, obs_cell, obs_value, obs_var, obs_noise):
    members_dev, planes_dev, plane_cells = ensemble.shape
    obs_dev = obs_cell.shape[0]
    slabs = lax.axis_size("space")
    mem_count = lax.axis_size("mem")
    members = members_dev * mem_count
    reach_slabs = min(8, slabs // 4)
    width = plane_cells // slabs
    state_rows = planes_dev * members_dev
    strips = width // LANES
    strip_rows, drive_rows = strips * state_rows, strips * planes_dev
    held_rows = round_up(strip_rows + drive_rows, SUBLANES)
    sent_rows = 2 * strip_rows + round_up(2 * drive_rows, SUBLANES)
    state_bytes = 4 * ensemble.size
    hops = slabs // 2
    sizes = dict(planes_dev=planes_dev, members_dev=members_dev)

    inputs = (ensemble, forcing, obs_cell[None], obs_value[None], obs_var[None], obs_noise)
    inputs = [pltpu.with_memory_space_constraint(x, pltpu.HBM) for x in inputs]
    give, keep, side, local = on_core(
        functools.partial(pack_kernel, count=len(inputs)),
        [
            (hops, held_rows, LANES),
            (hops, held_rows, LANES),
            (members_dev + SUBLANES, obs_dev),
            jax.ShapeDtypeStruct((1, obs_dev), jnp.int32),
        ],
        ensemble.size,
        2 * state_bytes,
        [pltpu.VMEM(x.shape, x.dtype) for x in inputs]
        + [pltpu.SemaphoreType.DMA((len(inputs),))],
        in_specs=[pl.BlockSpec(memory_space=pltpu.HBM)] * len(inputs),
    )(*inputs)
    got = flipped(give, "space", 1)
    sent = on_core(
        functools.partial(join_sent_kernel, state_rows=strip_rows, drive_rows=drive_rows),
        [(sent_rows, LANES)] * (hops - 1),
        1,
        2 * state_bytes,
    )(keep, got)
    come = [flipped(sent[n - 1], "space", 2 * n) for n in range(1, hops)]
    own, cross = on_core(
        functools.partial(forecast_kernel, slabs=slabs, **sizes),
        [(hops, state_rows, width)] * 2,
        24 * ensemble.size,
        2 * state_bytes,
        scratch=[pltpu.VMEM((slabs, held_rows, LANES), jnp.float32)],
    )(keep, got, *come)

    crossed = flipped(cross, "space", 1)
    back = on_core(join_kernel, [(2, state_rows, width)] * hops, 1, 2 * state_bytes)(own, crossed)
    home = back[0]
    pieces = [home] + [flipped(back[n], "space", 2 * n) for n in range(1, hops)]
    leading = [(0, 2), (3, 1), (1, 0), (2, 3)]
    trailing = [(0, 1), (3, 2), (1, 3), (2, 0)]
    outward = [(1, 0), (2, 3)]
    home_lead = lax.ppermute(home, "mem", leading)
    home_trail = lax.ppermute(home, "mem", trailing)
    observed, rest, whole = on_core(
        functools.partial(observe_kernel, plane_cells=plane_cells, **sizes),
        [
            (members_dev, obs_dev),
            (slabs - 2, state_rows, width),
            (slabs, state_rows, width),
        ],
        6 * ensemble.size * obs_dev,
        state_bytes,
    )(*pieces, local)

    seen = [observed] + [flipped(observed, "mem", n) for n in range(1, mem_count)]
    rest_lead = lax.ppermute(rest, "mem", leading)
    rest_trail = lax.ppermute(rest, "mem", trailing)
    block = on_core(
        stack_kernel, (members + members_dev + SUBLANES, obs_dev), 1, 8 * members * obs_dev
    )(*seen, side)
    near = [block] + [flipped(block, "space", 2 * n) for n in range(1, hops)]
    gathered = []
    for n in range(hops):
        gathered += [near[n], flipped(near[n], "space", 1)]

    all_middle = lax.ppermute(whole, "mem", [(1, 2), (2, 1)])
    passed = on_core(merge_kernel, (slabs, state_rows, width), 1, 2 * state_bytes)(
        home_lead, rest_lead
    )
    all_out = lax.ppermute(passed, "mem", outward)

    pair = 2
    tiles = slabs // pair
    near_tiles = min(tiles, 1 + 2 * (-(-reach_slabs // pair)))
    tile = pair * obs_dev
    count = slabs * obs_dev
    low_type = jnp.bfloat16
    gain = on_core(
        functools.partial(
            solve_kernel, members=members, pair=pair, reach_slabs=reach_slabs, **sizes
        ),
        (planes_dev, members_dev, members),
        6 * count * count * (members + 2 * ITERS * members_dev),
        4 * count * (members + members_dev),
        [
            pltpu.VMEM((slabs, 3 * members, obs_dev), low_type),
            pltpu.VMEM((slabs, obs_dev, 2 * members), low_type),
            pltpu.VMEM((slabs, SUBLANES, obs_dev), jnp.float32),
            pltpu.VMEM((tiles, near_tiles * tile, tile), low_type),
            pltpu.VMEM((tiles, near_tiles * tile, tile), low_type),
            pltpu.VMEM((slabs, members_dev, obs_dev), jnp.float32),
            pltpu.VMEM((slabs, members_dev, obs_dev), jnp.float32),
            pltpu.VMEM((slabs, members_dev, obs_dev), jnp.float32),
            pltpu.VMEM((2 * members_dev, count), low_type),
        ],
        room=20,
    )(*gathered)

    part, level = on_core(
        lambda *refs: early_kernel(refs[0:3], refs[3:6], *refs[6:]),
        [(slabs, state_rows, width), (slabs, SUBLANES, width)],
        4 * ensemble.size * members,
        4 * state_bytes,
        room=12,
    )(home, home_lead, home_trail, rest, rest_lead, rest_trail, gain)
    return on_core(
        update_kernel,
        ensemble.shape,
        2 * ensemble.size * members,
        4 * state_bytes,
        [
            pltpu.VMEM((slabs, members_dev, planes_dev, width), jnp.float32),
            pltpu.SemaphoreType.DMA((slabs,)),
        ],
        room=12,
        out_specs=pl.BlockSpec(memory_space=pltpu.HBM),
    )(part, level, all_middle, all_out, gain)


def shards(ensemble, forcing, obs_cell, obs_value, obs_var, obs_noise):
    args = (ensemble, forcing, obs_cell, obs_value, obs_var, obs_noise)
    members_dev, _, plane_cells = ensemble.shape
    slabs, groups, obs_dev = (lax.axis_size("space"), lax.axis_size("mem"), obs_cell.shape[0])
    aligned = (
        obs_dev % LANES == 0
        and plane_cells % (slabs * LANES) == 0
        and members_dev % SUBLANES == 0
        and (members_dev * groups) % LANES == 0
    )
    small = 4 * (slabs * obs_dev) ** 2 <= 2**24
    paired = slabs & (slabs - 1) == 0 and slabs >= 4
    if aligned and small and paired and groups == 4:
        return replicated(*args)
    return banded(*args)


def solution(mesh):
    placed = (
        P("mem", "space", None),
        P("space", None),
        P("space"),
        P("space"),
        P("space"),
        P("mem", "space"),
    )
    return jax.shard_map(
        shards, mesh=mesh, in_specs=placed, out_specs=P("mem", "space", None), check_vma=False
    )
```

```python
import functools

import jax
import jax.numpy as jnp
from jax import lax
from jax.experimental import pallas as pl
from jax.experimental.pallas import tpu as pltpu
from jax.sharding import PartitionSpec as P


FSTEPS = 4
ITERS = 6
LANES = 128
SUBLANES = 8

time_step = 0.05
highest = lax.Precision.HIGHEST


def from_behind(value, axis, steps):
    count = lax.axis_size(axis)
    pairs = [(source, (source + steps) % count) for source in range(count)]
    return lax.ppermute(value, axis, pairs)


def flipped(value, axis, mask):
    count = lax.axis_size(axis)
    return lax.ppermute(value, axis, [(i, i ^ mask) for i in range(count)])


def padded_2(x, sides, width):
    for axis, dim in sides:
        size, length = (lax.axis_size(axis), x.shape[dim])
        up = [(i, (i + 1) % size) for i in range(size)]
        down = [(j, i) for i, j in up]
        last = lax.slice_in_dim(x, length - width, length, axis=dim)
        initial = lax.slice_in_dim(x, 0, width, axis=dim)
        before = lax.ppermute(last, axis, up)
        after = lax.ppermute(initial, axis, down)
        x = jnp.concatenate([before, x, after], axis=dim)
    return x


def taper_of(planes_a, planes_b, planes_all, reach_planes):
    spread = jnp.abs(planes_a[:, None] - planes_b[None, :])
    spread = jnp.minimum(spread, planes_all - spread)
    return jnp.maximum(0.0, 1.0 - spread.astype(jnp.float32) / reach_planes)


def collect_band(values, along, reach_slabs):
    pieces = []
    for offset in range(-reach_slabs, reach_slabs + 1):
        if offset == 0:
            pieces.append(values)
        else:
            pieces.append(from_behind(values, "space", -offset))
    return jnp.concatenate(pieces, axis=along)


def banded(ensemble, forcing, obs_cell, obs_value, obs_var, obs_noise):
    members_dev, planes_dev, plane_cells = ensemble.shape
    obs_dev = obs_cell.shape[0]
    space_count = lax.axis_size("space")
    mem_count = lax.axis_size("mem")
    space_index = lax.axis_index("space")
    mem_index = lax.axis_index("mem")
    members = members_dev * mem_count
    planes_all = planes_dev * space_count
    reach_slabs = min(8, space_count // 4)
    reach_planes = planes_dev * reach_slabs
    band_width = reach_slabs * obs_dev
    states = ensemble
    for _ in range(FSTEPS):
        padded = padded_2(states, (("space", 1),), 2)
        forward_one = padded[:, 3 : 3 + planes_dev]
        back_one = padded[:, 1 : 1 + planes_dev]
        back_two = padded[:, 0:planes_dev]
        states = states + time_step * ((forward_one - back_two) * back_one - states + forcing)
    slab_cells = planes_dev * plane_cells
    local_cells = obs_cell - space_index * slab_cells
    observed = jnp.take(states.reshape(members_dev, slab_cells), local_cells, axis=1)
    own_planes = obs_cell // plane_cells
    own_rows = lax.all_gather(observed, "mem", axis=0, tiled=True)
    own_mean = jnp.sum(own_rows, axis=0) / members
    own_anom = own_rows - own_mean
    stacked = jnp.concatenate([own_anom, own_planes.astype(jnp.float32)[None, :]], axis=0)
    band = collect_band(stacked, 1, reach_slabs)
    context_anom = band[:members]
    context_planes = band[members].astype(jnp.int32)
    context_count = context_anom.shape[1]
    taper_block = taper_of(own_planes, context_planes, planes_all, reach_planes)
    gram_block = jnp.dot(own_anom.T, context_anom, precision=highest) / (members - 1)
    diagonal = jnp.arange(context_count)[None, :] == (band_width + jnp.arange(obs_dev))[:, None]
    covariance = taper_block * gram_block + jnp.where(diagonal, obs_var[:, None], 0.0)
    row_max = jnp.max(jnp.sum(jnp.abs(covariance), axis=1))
    var_min = jnp.min(obs_var)
    both = lax.pmax((row_max, -var_min), "space")
    upper_bound = both[0]
    lower_bound = -both[1]
    mean_rhs = obs_value - own_mean
    member_anom = lax.dynamic_slice_in_dim(own_anom, mem_index * members_dev, members_dev, 0)
    anom_rhs = (jnp.sqrt(obs_var)[None, :] * obs_noise - member_anom).T
    center = (upper_bound + lower_bound) / 2.0
    radius = (upper_bound - lower_bound) / 2.0
    sigma_ratio = center / radius
    rho_now = 1.0 / sigma_ratio
    resid_anom, resid_mean = (anom_rhs, mean_rhs)
    dir_anom, dir_mean = (anom_rhs / center, mean_rhs / center)
    anom_weight = jnp.zeros_like(anom_rhs)
    mean_weight = jnp.zeros_like(mean_rhs)
    for iteration in range(ITERS):
        anom_weight = anom_weight + dir_anom
        mean_weight = mean_weight + dir_mean
        if iteration < ITERS - 1:
            joined = jnp.concatenate([dir_anom, dir_mean[:, None]], axis=1)
            band_dirs = collect_band(joined, 0, reach_slabs)
            image = jnp.dot(covariance, band_dirs, precision=highest)
            image_anom = image[:, :-1]
            image_mean = image[:, -1]
            resid_anom = resid_anom - image_anom
            resid_mean = resid_mean - image_mean
            rho_next = 1.0 / (2.0 * sigma_ratio - rho_now)
            dir_anom = rho_next * rho_now * dir_anom + 2.0 * rho_next / radius * resid_anom
            dir_mean = rho_next * rho_now * dir_mean + 2.0 * rho_next / radius * resid_mean
            rho_now = rho_next
    weight = anom_weight + mean_weight[:, None]
    owned_cells = lax.all_to_all(states, "mem", split_axis=2, concat_axis=0, tiled=True)
    weight_rows = lax.all_gather(weight, "mem", axis=1, tiled=True)
    weight_context = collect_band(weight_rows, 0, reach_slabs)
    own_plane_ids = space_index * planes_dev + jnp.arange(planes_dev, dtype=jnp.int32)
    plane_taper = taper_of(own_plane_ids, context_planes, planes_all, reach_planes)

    def plane_gain(taper_row):
        return jnp.dot(context_anom * taper_row[None, :], weight_context, precision=highest)

    gain_blocks = lax.map(plane_gain, plane_taper)
    state_mean = jnp.sum(owned_cells, axis=0) / members
    state_anom = owned_cells - state_mean
    update = jnp.einsum("jxp,xjk->kxp", state_anom, gain_blocks, precision=highest) / (members - 1)
    analysis = owned_cells + update
    return lax.all_to_all(analysis, "mem", split_axis=0, concat_axis=2, tiled=True)


def halves(x):
    high = x.astype(jnp.bfloat16)
    low = (x - high.astype(jnp.float32)).astype(jnp.bfloat16)
    return high, low


def mxu(a, b):
    return jnp.dot(a, b, preferred_element_type=jnp.float32)


def round_up(value, unit):
    return -(-value // unit) * unit


def pack_kernel(*refs, count):
    sources, refs = refs[:count], refs[count:]
    give_ref, keep_ref, side_ref, local_ref, *targets, sems = refs
    copies = [
        pltpu.make_async_copy(source, target, sems.at[n])
        for n, (source, target) in enumerate(zip(sources, targets))
    ]
    for copy in copies:
        copy.start()
    ens_ref, forcing_ref, cell_ref, value_ref, var_ref, noise_ref = targets
    planes_dev, cells = forcing_ref.shape
    member_rows = planes_dev * cells // LANES
    members_dev = ens_ref.shape[0] // member_rows
    blocks, rows, _ = give_ref.shape
    strips = cells // (2 * blocks * LANES)
    state_rows = strips * planes_dev * members_dev
    me = lax.axis_index("space")
    for copy in copies[1:]:
        copy.wait()
    local = cell_ref[...] - me * (planes_dev * cells)
    local_ref[...] = local
    side_ref[:members_dev] = value_ref[...] + jnp.sqrt(var_ref[...]) * noise_ref[...]
    place = jnp.zeros(local.shape, jnp.float32) + (me * planes_dev).astype(jnp.float32)
    for plane in range(1, planes_dev):
        place = place + jnp.where(local >= plane * cells, 1.0, 0.0)
    fill = jnp.zeros((SUBLANES - 2, local.shape[1]), jnp.float32)
    side_ref[members_dev:] = jnp.concatenate([var_ref[...], place, fill], axis=0)
    copies[0].wait()
    tail = jnp.zeros((rows - state_rows - strips * planes_dev, LANES), jnp.float32)
    for hop in range(blocks):
        for ref, flip in ((give_ref, 1), (keep_ref, 0)):
            first = jnp.bitwise_xor(me, 2 * hop + flip) * strips
            drive = []
            for strip in range(strips):
                lanes = pl.ds(pl.multiple_of((first + strip) * LANES, LANES), LANES)
                for plane in range(planes_dev):
                    top = (strip * planes_dev + plane) * members_dev
                    row = (first + strip) * planes_dev + plane
                    values = ens_ref[pl.ds(row, members_dev, stride=member_rows), :]
                    ref[hop, top : top + members_dev, :] = values
                drive.append(forcing_ref[:, lanes])
            ref[hop, state_rows:, :] = jnp.concatenate(drive + [tail], axis=0)


def join_sent_kernel(keep_ref, got_ref, *outs, state_rows, drive_rows):
    both = (keep_ref, got_ref)
    for hop, out in enumerate(outs):
        for n, ref in enumerate(both):
            out[n * state_rows : (n + 1) * state_rows, :] = ref[hop + 1, :state_rows]
        drive = [ref[hop + 1, state_rows : state_rows + drive_rows] for ref in both]
        spare = out.shape[0] - 2 * (state_rows + drive_rows)
        if spare:
            drive.append(jnp.zeros((spare, LANES), jnp.float32))
        out[2 * state_rows :, :] = jnp.concatenate(drive, axis=0)


def join_kernel(keep_ref, got_ref, *outs):
    for hop, out in enumerate(outs):
        out[0] = keep_ref[hop]
        out[1] = got_ref[hop]


def forecast_kernel(*refs, planes_dev, members_dev, slabs):
    keep_ref, got_ref, others = refs[0], refs[1], refs[2 : 1 + slabs // 2]
    own_ref, cross_ref, grid_ref = refs[1 + slabs // 2 :]
    strips = own_ref.shape[2] // LANES
    strip_rows = planes_dev * members_dev
    state_rows, drive_rows = strips * strip_rows, strips * planes_dev
    count = slabs * planes_dev
    me = lax.axis_index("space")
    grid_ref[me] = keep_ref[0]
    grid_ref[jnp.bitwise_xor(me, 1)] = got_ref[0]
    for hop, other in enumerate(others):
        for flip in range(2):
            slab = jnp.bitwise_xor(me, 2 * hop + 2 + flip)
            grid_ref[slab, :state_rows] = other[flip * state_rows : (flip + 1) * state_rows]
            first = 2 * state_rows + flip * drive_rows
            grid_ref[slab, state_rows : state_rows + drive_rows] = other[first : first + drive_rows]
    for strip in range(strips):
        drive = []
        for plane in range(count):
            row = state_rows + strip * planes_dev + plane % planes_dev
            drive.append(grid_ref[plane // planes_dev, row : row + 1, :])
        for member in range(0, members_dev, SUBLANES):
            tops = [
                strip * strip_rows + (plane % planes_dev) * members_dev + member
                for plane in range(count)
            ]
            column = [
                grid_ref[plane // planes_dev, tops[plane] : tops[plane] + SUBLANES, :]
                for plane in range(count)
            ]
            for _ in range(FSTEPS):
                column = [
                    column[n]
                    + time_step
                    * (
                        (column[(n + 1) % count] - column[n - 2]) * column[n - 1]
                        - column[n]
                        + drive[n]
                    )
                    for n in range(count)
                ]
            for plane in range(count):
                top = tops[plane]
                grid_ref[plane // planes_dev, top : top + SUBLANES, :] = column[plane]
    for hop in range(slabs // 2):
        for ref, flip in ((own_ref, 0), (cross_ref, 1)):
            slab = jnp.bitwise_xor(me, 2 * hop + flip)
            for strip in range(strips):
                rows = slice(strip * strip_rows, (strip + 1) * strip_rows)
                ref[hop, :, strip * LANES : (strip + 1) * LANES] = grid_ref[slab, rows]


def collect_kernel(*refs):
    pieces, (rest_ref, whole_ref) = refs[:-2], refs[-2:]
    early = whole_ref.shape[0] - rest_ref.shape[0]
    first = 0
    for piece in pieces:
        values = piece[...]
        whole_ref[first : first + values.shape[0]] = values
        if first >= early:
            rest_ref[first - early : first - early + values.shape[0]] = values
        first += values.shape[0]


def observe_kernel(whole_ref, local_ref, out_ref, *, planes_dev, members_dev, plane_cells):
    blocks, _, width = whole_ref.shape
    obs_dev = local_ref.shape[1]
    me = lax.axis_index("space")
    local = local_ref[...]
    total = jnp.zeros((3 * members_dev, obs_dev), jnp.float32)
    for n in range(blocks):
        block = jnp.bitwise_xor(me, n)
        for plane in range(planes_dev):
            base = plane * plane_cells + block * width
            index = lax.broadcasted_iota(jnp.int32, (width, obs_dev), 0)
            pick = (index == local - base).astype(jnp.float32).astype(jnp.bfloat16)
            values = whole_ref[n, plane * members_dev : (plane + 1) * members_dev, :]
            high = values.astype(jnp.bfloat16)
            middle, low = halves(values - high.astype(jnp.float32))
            total += mxu(jnp.concatenate([high, middle, low], axis=0), pick)
    out_ref[...] = (
        total[:members_dev]
        + total[members_dev : 2 * members_dev]
        + total[2 * members_dev :]
    )


def stack_kernel(own_ref, one_ref, two_ref, three_ref, side_ref, out_ref):
    group = lax.axis_index("mem")
    mid = jnp.logical_and(group > 0, group < lax.axis_size("mem") - 1)
    one, two = one_ref[...], two_ref[...]
    ordered = (own_ref[...], jnp.where(mid, two, one), jnp.where(mid, one, two), three_ref[...])
    row = 0
    for values in (*ordered, side_ref[...]):
        out_ref[row : row + values.shape[0]] = values
        row += values.shape[0]


def solve_kernel(*refs, members, members_dev, planes_dev, pair, reach_slabs):
    slabs = len(refs) - 10
    ins, gain_ref = refs[:slabs], refs[slabs]
    anom_ref, flip_ref, side_ref, cov_hi, cov_lo, dir_ref, res_ref, sol_ref, split_ref = refs[
        slabs + 1 :
    ]
    obs_dev = ins[0].shape[1]
    planes_all = planes_dev * slabs
    reach_planes = planes_dev * reach_slabs
    me = lax.axis_index("space")
    member_count = jnp.float32(members)

    for offset in range(slabs):
        slab = jnp.bitwise_xor(me, offset)
        block = ins[offset][...]
        observed = block[:members]
        mean = jnp.sum(observed, axis=0, keepdims=True) / member_count
        anom = observed - mean
        high, low = halves(anom)
        anom_ref[slab, :members] = high
        anom_ref[slab, members : 2 * members] = high
        anom_ref[slab, 2 * members :] = low
        turned = anom.T
        turned_hi, turned_lo = halves(turned)
        flip_ref[slab, :, :members] = turned_hi
        flip_ref[slab, :, members:] = turned_lo
        res_ref[slab] = block[members : members + members_dev] - observed[:members_dev]
        side_ref[slab] = block[members + members_dev : members + members_dev + SUBLANES]

    lower = None
    variances, places, columns = [], [], []
    for slab in range(slabs):
        side = side_ref[slab]
        variances.append(side[0:1])
        places.append(side[1:2])
        columns.append(side.T[:, 1:2])
    var_row = jnp.concatenate(variances, axis=1)
    place_row = jnp.concatenate(places, axis=1)
    lower = jnp.min(var_row, axis=1, keepdims=True)

    tile = pair * obs_dev
    tiles = slabs // pair
    reach_tiles = -(-reach_slabs // pair)
    near = {}
    for right in range(tiles):
        near[right] = sorted({(right + step) % tiles for step in range(-reach_tiles, reach_tiles + 1)})
    scale = jnp.float32(1.0 / (members - 1))
    upper = None
    for right in range(tiles):
        span = slice(right * tile, (right + 1) * tile)
        tops = jnp.concatenate(
            [anom_ref[right * pair + n, : 2 * members] for n in range(pair)], axis=1
        )
        lows = jnp.concatenate(
            [anom_ref[right * pair + n, 2 * members :] for n in range(pair)], axis=1
        )
        along = place_row[:, span]
        sums = None
        for order, left in enumerate(near[right]):
            for part in range(pair):
                slab = left * pair + part
                rows = flip_ref[slab]
                gram = mxu(rows, tops) + mxu(rows[:, :members], lows)
                spread = jnp.abs(columns[slab] - along)
                spread = jnp.minimum(spread, planes_all - spread)
                taper = jnp.maximum(0.0, 1.0 - spread / reach_planes)
                cov = taper * (gram * scale)
                if left == right:
                    below = lax.broadcasted_iota(jnp.int32, (obs_dev, tile), 0) + part * obs_dev
                    across = lax.broadcasted_iota(jnp.int32, (obs_dev, tile), 1)
                    cov = cov + jnp.where(below == across, var_row[:, span], 0.0)
                size = jnp.sum(jnp.abs(cov), axis=0, keepdims=True)
                sums = size if sums is None else sums + size
                high, low = halves(cov)
                top = (order * pair + part) * obs_dev
                cov_hi[right, top : top + obs_dev, :] = high
                cov_lo[right, top : top + obs_dev, :] = low
        biggest = jnp.max(sums, axis=1, keepdims=True)
        upper = biggest if upper is None else jnp.maximum(upper, biggest)

    center = (upper + lower) / 2.0
    radius = (upper - lower) / 2.0
    sigma_ratio = center / radius
    rho_now = 1.0 / sigma_ratio
    for slab in range(slabs):
        span = slice(slab * obs_dev, (slab + 1) * obs_dev)
        start = res_ref[slab] / center
        dir_ref[slab] = start
        sol_ref[slab] = start
        high, low = halves(start)
        split_ref[:members_dev, span] = high
        split_ref[members_dev:, span] = low
    for iteration in range(ITERS - 1):
        rho_next = 1.0 / (2.0 * sigma_ratio - rho_now)
        keep = rho_next * rho_now
        take = 2.0 * rho_next / radius
        images = []
        for right in range(tiles):
            lefts = jnp.concatenate(
                [split_ref[:, left * tile : (left + 1) * tile] for left in near[right]], axis=1
            )
            both = mxu(lefts, cov_hi[right])
            images.append(
                both[:members_dev]
                + both[members_dev:]
                + mxu(lefts[:members_dev], cov_lo[right])
            )
        for slab in range(slabs):
            span = slice(slab * obs_dev, (slab + 1) * obs_dev)
            part = slab % pair
            image = images[slab // pair][:, part * obs_dev : (part + 1) * obs_dev]
            residual = res_ref[slab] - image
            res_ref[slab] = residual
            ahead = keep * dir_ref[slab] + take * residual
            dir_ref[slab] = ahead
            sol_ref[slab] += ahead
            if iteration < ITERS - 2:
                high, low = halves(ahead)
                split_ref[:members_dev, span] = high
                split_ref[members_dev:, span] = low
        rho_now = rho_next

    total = jnp.zeros((2 * planes_dev * members_dev, members), jnp.float32)
    extra = jnp.zeros((planes_dev * members_dev, members), jnp.float32)
    for slab in range(slabs):
        weight = sol_ref[slab]
        tapered = []
        for plane in range(planes_dev):
            own = (me * planes_dev + plane).astype(jnp.float32)
            spread = jnp.abs(own - place_row[:, slab * obs_dev : (slab + 1) * obs_dev])
            spread = jnp.minimum(spread, planes_all - spread)
            tapered.append(weight * jnp.maximum(0.0, 1.0 - spread / reach_planes))
        high, low = halves(jnp.concatenate(tapered, axis=0))
        rows = flip_ref[slab]
        total += mxu(jnp.concatenate([high, low], axis=0), rows[:, :members])
        extra += mxu(high, rows[:, members:])
    half = planes_dev * members_dev
    gain = (total[:half] + total[half:] + extra) * scale
    for plane in range(planes_dev):
        gain_ref[plane] = gain[plane * members_dev : (plane + 1) * members_dev]


def centred(gain_ref, plane):
    gain = gain_ref[plane]
    return halves(gain - jnp.mean(gain, axis=1, keepdims=True))


def early_kernel(home_refs, rest_refs, gain_ref, part_ref, level_ref):
    blocks, _, _ = part_ref.shape
    planes_dev, members_dev = gain_ref.shape[:2]
    split = home_refs[0].shape[0]
    here = len(home_refs) * members_dev
    for plane in range(planes_dev):
        high, low = centred(gain_ref, plane)
        high, low = high[:, :here], low[:, :here]
        both = jnp.concatenate([high, low], axis=0)
        span = slice(plane * members_dev, (plane + 1) * members_dev)
        for block in range(blocks):
            refs, part = (home_refs, block) if block < split else (rest_refs, block - split)
            parts = [ref[part, span, :] for ref in refs]
            values = jnp.concatenate(parts, axis=0)
            level = jnp.sum(values, axis=0, keepdims=True) / jnp.float32(here)
            anom_hi, anom_lo = halves(values - level)
            change = mxu(both, anom_hi)
            change = change[:members_dev] + change[members_dev:] + mxu(high, anom_lo)
            part_ref[block, span, :] = parts[0] + change
            level_ref[block, plane : plane + 1, :] = level


def update_kernel(part_ref, level_ref, middle_ref, outer_ref, gain_ref, out_hbm, out_ref, sems):
    blocks, _, width = part_ref.shape
    members_dev, planes_dev = out_hbm.shape[:2]
    me = lax.axis_index("space")
    factors = []
    for plane in range(planes_dev):
        high, low = centred(gain_ref, plane)
        high, low = high[:, -members_dev:], low[:, -members_dev:]
        factors.append((high, jnp.concatenate([high, low], axis=0)))
    copies = []
    for block in range(blocks):
        for plane in range(planes_dev):
            high, both = factors[plane]
            span = slice(plane * members_dev, (plane + 1) * members_dev)
            values = middle_ref[block, span, :] + outer_ref[block, span, :]
            anom_hi, anom_lo = halves(values - level_ref[block, plane : plane + 1, :])
            change = mxu(both, anom_hi)
            change = change[:members_dev] + change[members_dev:] + mxu(high, anom_lo)
            out_ref[block, :, plane, :] = part_ref[block, span, :] + change
        start = jnp.bitwise_xor(me, block) * width
        target = out_hbm.at[:, :, pl.ds(pl.multiple_of(start, width), width)]
        copies.append(pltpu.make_async_copy(out_ref.at[block], target, sems.at[block]))
        copies[-1].start()
    for copy in copies:
        copy.wait()


def merge_kernel(home_ref, rest_ref, out_ref):
    split = home_ref.shape[0]
    out_ref[:split] = home_ref[...]
    out_ref[split:] = rest_ref[...]


def on_core(kernel, shapes, flops, moved, scratch=(), room=8, **extra):
    single = not isinstance(shapes, list)
    many = [shapes] if single else shapes
    out = [x if hasattr(x, "dtype") else jax.ShapeDtypeStruct(x, jnp.float32) for x in many]
    return pl.pallas_call(
        kernel,
        compiler_params=pltpu.CompilerParams(vmem_limit_bytes=room * 2**20),
        out_shape=out[0] if single else out,
        scratch_shapes=list(scratch),
        cost_estimate=pl.CostEstimate(flops=flops, bytes_accessed=moved, transcendentals=0),
        **extra,
    )


def replicated(ensemble, forcing, obs_cell, obs_value, obs_var, obs_noise):
    members_dev, planes_dev, plane_cells = ensemble.shape
    obs_dev = obs_cell.shape[0]
    slabs = lax.axis_size("space")
    mem_count = lax.axis_size("mem")
    members = members_dev * mem_count
    reach_slabs = min(8, slabs // 4)
    width = plane_cells // slabs
    state_rows = planes_dev * members_dev
    strips = width // LANES
    strip_rows, drive_rows = strips * state_rows, strips * planes_dev
    held_rows = round_up(strip_rows + drive_rows, SUBLANES)
    sent_rows = 2 * strip_rows + round_up(2 * drive_rows, SUBLANES)
    state_bytes = 4 * ensemble.size
    hops = slabs // 2
    sizes = dict(planes_dev=planes_dev, members_dev=members_dev)

    rows = ensemble.reshape(members_dev, planes_dev, -1, LANES)
    rows = rows.transpose(0, 2, 1, 3).reshape(-1, LANES)
    inputs = (rows, forcing, obs_cell[None], obs_value[None], obs_var[None], obs_noise)
    inputs = [pltpu.with_memory_space_constraint(x, pltpu.HBM) for x in inputs]
    give, keep, side, local = on_core(
        functools.partial(pack_kernel, count=len(inputs)),
        [
            (hops, held_rows, LANES),
            (hops, held_rows, LANES),
            (members_dev + SUBLANES, obs_dev),
            jax.ShapeDtypeStruct((1, obs_dev), jnp.int32),
        ],
        ensemble.size,
        2 * state_bytes,
        [pltpu.VMEM(x.shape, x.dtype) for x in inputs]
        + [pltpu.SemaphoreType.DMA((len(inputs),))],
        in_specs=[pl.BlockSpec(memory_space=pltpu.HBM)] * len(inputs),
    )(*inputs)
    got = flipped(give, "space", 1)
    sent = on_core(
        functools.partial(join_sent_kernel, state_rows=strip_rows, drive_rows=drive_rows),
        [(sent_rows, LANES)] * (hops - 1),
        1,
        2 * state_bytes,
    )(keep, got)
    come = [flipped(sent[n - 1], "space", 2 * n) for n in range(1, hops)]
    own, cross = on_core(
        functools.partial(forecast_kernel, slabs=slabs, **sizes),
        [(hops, state_rows, width)] * 2,
        24 * ensemble.size,
        2 * state_bytes,
        scratch=[pltpu.VMEM((slabs, held_rows, LANES), jnp.float32)],
    )(keep, got, *come)

    crossed = flipped(cross, "space", 1)
    back = on_core(join_kernel, [(2, state_rows, width)] * hops, 1, 2 * state_bytes)(own, crossed)
    home = back[0]
    pieces = [home] + [flipped(back[n], "space", 2 * n) for n in range(1, hops)]
    leading = [(0, 2), (3, 1), (1, 0), (2, 3)]
    trailing = [(0, 1), (3, 2), (1, 3), (2, 0)]
    outward = [(1, 0), (2, 3)]
    home_lead = lax.ppermute(home, "mem", leading)
    home_trail = lax.ppermute(home, "mem", trailing)
    rest, whole = on_core(
        collect_kernel,
        [(slabs - 2, state_rows, width), (slabs, state_rows, width)],
        1,
        3 * state_bytes,
    )(*pieces)
    rest_lead = lax.ppermute(rest, "mem", leading)
    observed = on_core(
        functools.partial(observe_kernel, plane_cells=plane_cells, **sizes),
        (members_dev, obs_dev),
        6 * ensemble.size * obs_dev,
        state_bytes,
    )(whole, local)

    seen = [observed] + [flipped(observed, "mem", n) for n in range(1, mem_count)]
    rest_trail = lax.ppermute(rest, "mem", trailing)
    block = on_core(
        stack_kernel, (members + members_dev + SUBLANES, obs_dev), 1, 8 * members * obs_dev
    )(*seen, side)
    near = [block] + [flipped(block, "space", 2 * n) for n in range(1, hops)]
    gathered = []
    for n in range(hops):
        gathered += [near[n], flipped(near[n], "space", 1)]

    all_middle = lax.ppermute(whole, "mem", [(1, 2), (2, 1)])
    passed = on_core(merge_kernel, (slabs, state_rows, width), 1, 2 * state_bytes)(
        home_lead, rest_lead
    )
    all_out = lax.ppermute(passed, "mem", outward)

    pair = 2
    tiles = slabs // pair
    near_tiles = min(tiles, 1 + 2 * (-(-reach_slabs // pair)))
    tile = pair * obs_dev
    count = slabs * obs_dev
    low_type = jnp.bfloat16
    gain = on_core(
        functools.partial(
            solve_kernel, members=members, pair=pair, reach_slabs=reach_slabs, **sizes
        ),
        (planes_dev, members_dev, members),
        6 * count * count * (members + 2 * ITERS * members_dev),
        4 * count * (members + members_dev),
        [
            pltpu.VMEM((slabs, 3 * members, obs_dev), low_type),
            pltpu.VMEM((slabs, obs_dev, 2 * members), low_type),
            pltpu.VMEM((slabs, SUBLANES, obs_dev), jnp.float32),
            pltpu.VMEM((tiles, near_tiles * tile, tile), low_type),
            pltpu.VMEM((tiles, near_tiles * tile, tile), low_type),
            pltpu.VMEM((slabs, members_dev, obs_dev), jnp.float32),
            pltpu.VMEM((slabs, members_dev, obs_dev), jnp.float32),
            pltpu.VMEM((slabs, members_dev, obs_dev), jnp.float32),
            pltpu.VMEM((2 * members_dev, count), low_type),
        ],
        room=20,
    )(*gathered)

    part, level = on_core(
        lambda *refs: early_kernel(refs[0:3], refs[3:6], *refs[6:]),
        [(slabs, state_rows, width), (slabs, SUBLANES, width)],
        4 * ensemble.size * members,
        4 * state_bytes,
        room=12,
    )(home, home_lead, home_trail, rest, rest_lead, rest_trail, gain)
    return on_core(
        update_kernel,
        ensemble.shape,
        2 * ensemble.size * members,
        4 * state_bytes,
        [
            pltpu.VMEM((slabs, members_dev, planes_dev, width), jnp.float32),
            pltpu.SemaphoreType.DMA((slabs,)),
        ],
        room=12,
        out_specs=pl.BlockSpec(memory_space=pltpu.HBM),
    )(part, level, all_middle, all_out, gain)


def shards(ensemble, forcing, obs_cell, obs_value, obs_var, obs_noise):
    args = (ensemble, forcing, obs_cell, obs_value, obs_var, obs_noise)
    members_dev, _, plane_cells = ensemble.shape
    slabs, groups, obs_dev = (lax.axis_size("space"), lax.axis_size("mem"), obs_cell.shape[0])
    aligned = (
        obs_dev % LANES == 0
        and plane_cells % (slabs * LANES) == 0
        and members_dev % SUBLANES == 0
        and (members_dev * groups) % LANES == 0
    )
    small = 4 * (slabs * obs_dev) ** 2 <= 2**24
    paired = slabs & (slabs - 1) == 0 and slabs >= 4
    if aligned and small and paired and groups == 4:
        return replicated(*args)
    return banded(*args)


def solution(mesh):
    placed = (
        P("mem", "space", None),
        P("space", None),
        P("space"),
        P("space"),
        P("space"),
        P("mem", "space"),
    )
    return jax.shard_map(
        shards, mesh=mesh, in_specs=placed, out_specs=P("mem", "space", None), check_vma=False
    )
```
